32 devices in a mesh: dp: 4 (over y, x), tp: 8 (over z, core).
Axes of the slice: x: 2, y: 2, z: 4, core: 2. Of those that a mesh axis runs over, the one named last changes fastest.
Arguments:
- hidden_in: bfloat16 [4, 32, 4096], P(None, 'dp'), may hold values from -6 to 6
- pre_gain: float32 [4096], replicated, may hold values from 0.25 to 1.75
- w_zx: bfloat16 [4096, 2, 8192], P(None, None, 'tp'), may hold values from -0.09375 to 0.09375
- zx_codes: bfloat16 [4096, 2, 8192], P(('dp', 'tp')), may hold values from -4 to 4
- zx_exponents: int32 [32, 2, 64], P('dp', None, 'tp'), may hold values from -9 to -6
- w_bc: bfloat16 [4096, 2048], P(None, 'tp'), may hold values from -0.09375 to 0.09375
- w_dt: bfloat16 [4096, 128], P(None, 'tp'), may hold values from -0.09375 to 0.09375
- conv_x: float32 [5, 8192], P(None, 'tp'), may hold values from -0.6 to 0.6
- conv_bc: float32 [5, 2048], P(None, 'tp'), may hold values from -0.6 to 0.6
- dt_bias: float32 [128], P('tp'), may hold values from -2 to 0.5
- decay_rate: float32 [128], P('tp'), may hold values from 0.05 to 2
- skip_gain: float32 [128], P('tp'), may hold values from 0.5 to 1.5
- conv_state_x: bfloat16 [32, 3, 8192], P('dp', None, 'tp'), may hold values from -6 to 6
- conv_state_bc: bfloat16 [32, 3, 2048], P('dp', None, 'tp'), may hold values from -6 to 6
- ssm_state: float32 [32, 128, 64, 256], P('dp', 'tp'), may hold values from -6 to 6
- norm_gain: float32 [8192], P('tp'), may hold values from 0.25 to 1.75
- w_out: bfloat16 [8192, 4096], P('tp'), may hold values from -0.0625 to 0.0625
- out_codes: bfloat16 [8192, 4096], P('tp', 'dp'), may hold values from -4 to 4
- out_exponents: int32 [64, 32], P('tp', 'dp'), may hold values from -7 to -4
Outputs:
- mixed: bfloat16 [4, 32, 4096], P(None, 'dp', 'tp')
- final_state: float32 [32, 128, 64, 256], P('dp', 'tp')
The draws below stay inside these ranges and needn't reach their ends.
All inputs are finite; a program needn't handle non-finite values.
Results may differ from the reference program's by a relative error of at most 0.014.
Values may be sent and summed in bfloat16 or wider, within the bound.
A program may use at most 192 MiB of HBM per device.

```python
import math
import jax
import jax.numpy as jnp
from jax import lax

D = 4096
H = 128
P_SIZE = 64
N = 256
G = 4
BLK = 128
STEPS = 4
DI = 8192
ROWS = 32


def set_ends(drawn, own_key, smallest, top_value):
    longest = drawn.shape.index(max(drawn.shape))
    spots = []
    for shift in (0, 1):
        where = [jax.random.randint(jax.random.fold_in(own_key, axis), (), 0, length) for axis, length in enumerate(drawn.shape)]
        where[longest] = (where[longest] + shift) % drawn.shape[longest]
        spots.append(tuple(where))
    return drawn.at[spots[0]].set(smallest).at[spots[1]].set(top_value)


def block_scale(rng, dims, shards, smallest, top_value):
    loudness, own = 1.0, jax.random.fold_in(rng, 6)
    for dim, blocks in shards:
        draws = jnp.exp(jax.random.uniform(jax.random.fold_in(own, dim), (blocks,), jnp.float32, smallest / len(shards), top_value / len(shards)))
        loudness = loudness * jnp.repeat(draws, dims[dim] // blocks).reshape([-1 if axis == dim else 1 for axis in range(len(dims))])
    return loudness


def bell_draw(own_key, dims, width, bound, split=(), held_as=jnp.bfloat16):
    gain = block_scale(own_key, dims, split, -0.22, 0.18) if split else 1.0
    array = jax.random.normal(own_key, dims, jnp.float32) * width * gain
    return jnp.minimum(jnp.maximum(array, -bound), bound).astype(held_as)


def setup_inputs(seed: int = 0) -> dict:
    seeds = jax.random.split(jax.random.key(seed), 20)
    return {
        "hidden_in": bell_draw(seeds[0], (STEPS, ROWS, D), 1.0, 6.0, ((1, 4),)),
        "pre_gain": jnp.clip(1.0 + 0.15 * jax.random.normal(seeds[1], (D,), jnp.float32), 0.25, 1.75),
        "w_zx": bell_draw(seeds[2], (D, 2, DI), D ** -0.5, 0.09375, ((2, 8),)),
        "zx_codes": bell_draw(seeds[3], (D, 2, DI), 1.0, 4.0, ((0, 32),)),
        "zx_exponents": set_ends(jax.random.randint(seeds[4], (D // BLK, 2, DI // BLK), -9, -5), jax.random.fold_in(seeds[4], 1), -9, (-5) - 1).astype(jnp.int32),
        "w_bc": bell_draw(seeds[5], (D, 2 * G * N), D ** -0.5, 0.09375, ((1, 8),)),
        "w_dt": bell_draw(seeds[6], (D, H), D ** -0.5, 0.09375, ((1, 8),)),
        "conv_x": jnp.clip(jax.random.uniform(seeds[7], (5, DI), jnp.float32, -0.6, 0.6) * block_scale(seeds[7], (5, DI), ((1, 8),), -0.4, 0.0), -0.6, 0.6),
        "conv_bc": jnp.clip(jax.random.uniform(seeds[8], (5, 2 * G * N), jnp.float32, -0.6, 0.6) * block_scale(seeds[8], (5, 2 * G * N), ((1, 8),), -0.4, 0.0), -0.6, 0.6),
        "dt_bias": jnp.clip(-2.0 + 2.5 * jax.random.uniform(seeds[9], (H,), jnp.float32) ** block_scale(seeds[9], (H,), ((0, 8),), -0.2, 0.2), -2.0, 0.5),
        "decay_rate": jnp.clip(jnp.exp(math.log(2.0) - 3.6888794 * jax.random.uniform(seeds[10], (H,), jnp.float32) ** block_scale(seeds[10], (H,), ((0, 8),), -0.2, 0.2)), 0.05, 2.0),
        "skip_gain": jnp.clip(0.5 + 1.0 * jax.random.uniform(seeds[11], (H,), jnp.float32) ** block_scale(seeds[11], (H,), ((0, 8),), -0.2, 0.2), 0.5, 1.5),
        "conv_state_x": bell_draw(seeds[12], (ROWS, 3, DI), 1.0, 6.0, ((0, 4), (2, 8))),
        "conv_state_bc": bell_draw(seeds[13], (ROWS, 3, 2 * G * N), 1.0, 6.0, ((0, 4), (2, 8))),
        "ssm_state": bell_draw(seeds[14], (ROWS, H, P_SIZE, N), 1.0, 6.0, ((0, 4), (1, 8)), jnp.float32),
        "norm_gain": jnp.clip(1.0 + 0.15 * jax.random.normal(seeds[15], (DI,), jnp.float32), 0.25, 1.75),
        "w_out": bell_draw(seeds[16], (DI, D), DI ** -0.5, 0.0625, ((0, 8),)),
        "out_codes": bell_draw(seeds[17], (DI, D), 1.0, 4.0, ((0, 8), (1, 4))),
        "out_exponents": set_ends(jax.random.randint(seeds[18], (DI // BLK, D // BLK), -7, -3), jax.random.fold_in(seeds[18], 1), -7, (-3) - 1).astype(jnp.int32),
    }


EPS = 1e-05

def decode_pairs(codes, exponents, block):
    rows, pair, cols = codes.shape
    blocked = codes.astype(jnp.float32).reshape(rows // block, block, pair, cols // block, block)
    scales = jnp.exp2(exponents.astype(jnp.float32))
    return (blocked * scales[:, None, :, :, None]).reshape(rows, pair, cols)

def decode_matrix(codes, exponents, block):
    rows, cols = codes.shape
    blocked = codes.astype(jnp.float32).reshape(rows // block, block, cols // block, block)
    scales = jnp.exp2(exponents.astype(jnp.float32))
    return (blocked * scales[:, None, :, None]).reshape(rows, cols)

def conv_step(history, fresh, params):
    window = jnp.concatenate([history, fresh[:, None, :]], axis=1)
    mixed = lax.optimization_barrier(jnp.sum(window * params[:4][None], axis=1)) + params[4]
    return (jax.nn.silu(mixed), window[:, 1:])

def reference(hidden_in, pre_gain, w_zx, zx_codes, zx_exponents, w_bc, w_dt, conv_x, conv_bc, dt_bias, decay_rate, skip_gain, conv_state_x, conv_state_bc, ssm_state, norm_gain, w_out, out_codes, out_exponents):
    new_zx = (w_zx.astype(jnp.float32) + decode_pairs(zx_codes, zx_exponents, BLK)).astype(jnp.bfloat16)
    new_out = (w_out.astype(jnp.float32) + decode_matrix(out_codes, out_exponents, BLK)).astype(jnp.bfloat16)
    zx_flat = new_zx.reshape(D, 2 * DI)
    history_x = conv_state_x.astype(jnp.float32)
    history_bc = conv_state_bc.astype(jnp.float32)
    state = ssm_state
    results = []
    for step in range(STEPS):
        x = hidden_in[step].astype(jnp.float32)
        if step > 0:
            x = x + results[-1].astype(jnp.float32)
        rows = x.shape[0]
        normed = (x * lax.rsqrt(lax.optimization_barrier(jnp.mean(x * x, -1, keepdims=True)) + EPS) * pre_gain).astype(jnp.bfloat16)
        zx = jnp.dot(normed, zx_flat, preferred_element_type=jnp.float32).reshape(rows, 2, DI)
        gate = zx[:, 0]
        inner = zx[:, 1]
        bc_raw = jnp.dot(normed, w_bc, preferred_element_type=jnp.float32)
        dt_raw = jnp.dot(normed, w_dt, preferred_element_type=jnp.float32)
        conv_inner, history_x = conv_step(history_x, inner, conv_x)
        conv_state_out, history_bc = conv_step(history_bc, bc_raw, conv_bc)
        b_heads = jnp.repeat(conv_state_out[:, :G * N].reshape(rows, G, N), H // G, axis=1)
        c_heads = jnp.repeat(conv_state_out[:, G * N:].reshape(rows, G, N), H // G, axis=1)
        step_size = jax.nn.softplus(dt_raw + dt_bias)
        decay = jnp.exp(-step_size * decay_rate)
        inner_heads = conv_inner.reshape(rows, H, P_SIZE)
        state = decay[:, :, None, None] * state + (step_size[:, :, None] * inner_heads)[:, :, :, None] * b_heads[:, :, None, :]
        read = jnp.einsum('rhpn,rhn->rhp', state, c_heads, precision=lax.Precision.HIGHEST) + skip_gain[:, None] * inner_heads
        gated = (read.reshape(rows, DI) * jax.nn.silu(gate)).reshape(rows, G, DI // G)
        grouped = gated * lax.rsqrt(lax.optimization_barrier(jnp.mean(gated * gated, -1, keepdims=True)) + EPS)
        scaled = (grouped.reshape(rows, DI) * norm_gain).astype(jnp.bfloat16)
        results.append(jnp.dot(scaled, new_out, preferred_element_type=jnp.float32).astype(jnp.bfloat16))
    return (jnp.stack(results), state)
```

```python
import jax
import jax.numpy as jnp
from jax import lax
from jax.experimental import pallas as pl
from jax.experimental.pallas import tpu as pltpu
from jax.sharding import PartitionSpec as P

G = 4
BLK = 128
LANES = 128
EPS = 1e-05
MESH = pl.DeviceIdType.MESH
F32 = jnp.float32
BF16 = jnp.bfloat16


def silu(v):
    return v / (1.0 + jnp.exp(-v))


def make_kernel(ndp, ntp, steps, rows, dc, lc, cb, heads, psize, nstate, gsz, feats, di):
    oc = feats // ntp
    ac = dc // ntp
    nchunk = lc // LANES
    hpc = LANES // psize
    rpd = dc // ntp
    nt2 = ntp // 2
    nb = G * nstate // cb
    per = nstate // cb
    allr = ndp * rows
    nkb = dc // BLK

    def kernel(
        hid_hbm, gain_hbm, wdt_hbm, sc_hbm, so_hbm, ocodes_hbm, convx_hbm, convb_hbm, dtb_hbm,
        rate_hbm, skip_hbm, ng_hbm, hx0_hbm, hb0_hbm, state_hbm, codes_hbm, wzx_hbm, wbc_hbm,
        wout_hbm,
        out_ref, coef_ref, bst_ref,
        state, sb, hx, hb, hown, hrecv, hp, gp, d1s, d1r, d2s, d2r, s2, r2, cs, cr, gs, gr, qs, qr,
        os, orv, ags, agr, xr, mr,
        cv, wv, wbc, wo, sc_all, scs,
        gain_ref, gain_c, wdt_in, wdt_ref, so_in, so_ref, ocodes_ref, convx_ref, convb_ref,
        dtb_ref, rate_ref, skip_ref, ng_ref, hx0_ref, hb0_ref,
        l_sems, w_sems, cl_sem, st_sem, send_sem, v_sem, sc_sem, h_sem, d1_sem, d2_sem, sem2, c_sem,
        g_sem, q_sem, o_sem, a_sem, x_sem, f_sem,
    ):
        dp = lax.axis_index("dp")
        tp = lax.axis_index("tp")
        core = lax.rem(tp, 2)
        tp0 = tp - core
        mine = tp // 2
        sib = tp ^ 1
        pending = []

        def remote(src, dst, rsem, d, t):
            return pltpu.make_async_remote_copy(
                src_ref=src, dst_ref=dst, send_sem=send_sem, recv_sem=rsem,
                device_id=(d, t), device_id_type=MESH,
            )

        def send(src, dst, rsem, d, t):
            copy = remote(src, dst, rsem, d, t)
            copy.start()
            pending.append(copy)

        def recv(src, dst, rsem):
            remote(src, dst, rsem, dp, tp).wait_recv()

        def chunk(i):
            return pl.ds(pl.multiple_of(i * dc, LANES), dc)

        def columns(ti, par, ct):
            return pl.ds(pl.multiple_of((2 * ti + par) * lc + ct * LANES, LANES), LANES)

        small_loads = [
            (hid_hbm, hown), (hid_hbm.at[:, :, chunk(dp)], hrecv.at[dp]),
            (gain_hbm, gain_ref), (gain_hbm.at[:, chunk(dp)], gain_c),
            (sc_hbm, sc_all.at[mine]), (wdt_hbm, wdt_in), (so_hbm, so_in),
            (convx_hbm, convx_ref), (convb_hbm, convb_ref), (dtb_hbm, dtb_ref),
            (rate_hbm, rate_ref), (skip_hbm, skip_ref), (ng_hbm, ng_ref), (hx0_hbm, hx0_ref),
            (hb0_hbm, hb0_ref),
        ]
        small_loads = [
            pltpu.make_async_copy(a, b, l_sems.at[i]) for i, (a, b) in enumerate(small_loads)
        ]
        for copy in small_loads:
            copy.start()
        own_codes = []
        for k in list(range(1, nt2)) + [0]:
            ti = lax.rem(mine + k, nt2)
            for ct in range(nchunk):
                copy = pltpu.make_async_copy(
                    codes_hbm.at[:, :, columns(ti, core, ct)], cv.at[ti, core, ct],
                    cl_sem.at[k, ct],
                )
                copy.start()
                own_codes.append(copy)
        load_bc = pltpu.make_async_copy(wbc_hbm, wbc, w_sems.at[0])
        load_bc.start()

        barrier = pltpu.get_barrier_semaphore()
        for i in range(ndp):
            for j in range(ntp):
                if i + j > 0:
                    pl.semaphore_signal(
                        barrier, inc=1,
                        device_id=(lax.rem(dp + i, ndp), lax.rem(tp + j, ntp)),
                        device_id_type=MESH,
                    )
        pl.semaphore_wait(barrier, ndp * ntp - 1)

        for k in range(1, nt2):
            ti = lax.rem(mine + k, nt2)
            send(sc_hbm, sc_all.at[mine], sc_sem.at[k], dp, 2 * ti + core)
        for k in range(1, ndp):
            peer = lax.rem(dp + k, ndp)
            send(hid_hbm.at[:, :, chunk(peer)], hrecv.at[dp], h_sem.at[k], peer, tp)
        for k in list(range(1, nt2)) + [0]:
            ti = lax.rem(mine + k, nt2)
            for ct in range(nchunk):
                send(
                    codes_hbm.at[:, :, columns(ti, 1 - core, ct)], cv.at[ti, core, ct],
                    v_sem.at[k, ct], dp, sib,
                )
        load_w = []
        for ct in range(nchunk):
            copy = pltpu.make_async_copy(
                wzx_hbm.at[pl.ds(dp * dc, dc), :, pl.ds(ct * LANES, LANES)], wv.at[ct],
                w_sems.at[1 + ct],
            )
            copy.start()
            load_w.append(copy)
        load_st = []
        for r in range(rows):
            copy = pltpu.make_async_copy(state_hbm.at[r], state.at[r], st_sem.at[r])
            copy.start()
            load_st.append(copy)
        load_out = pltpu.make_async_copy(
            wout_hbm.at[:, pl.ds(pl.multiple_of(dp * dc, LANES), dc)], wo, w_sems.at[1 + nchunk]
        )
        load_out.start()
        load_oc = pltpu.make_async_copy(ocodes_hbm, ocodes_ref, w_sems.at[2 + nchunk])
        load_oc.start()

        for copy in small_loads:
            copy.wait()
        wdt_ref[...] = jnp.concatenate(
            [wdt_in[...].astype(F32), jnp.zeros((LANES - heads, feats), F32)], axis=0
        ).astype(BF16)
        hx[0:3] = hx0_ref[...].astype(F32)
        hb[0:3] = hb0_ref[...].astype(F32)
        power = jnp.exp2(so_in[...].astype(F32))
        for b in range(lc // BLK):
            so_ref[b] = jnp.concatenate(
                [jnp.broadcast_to(power[b, :, c : c + 1], (1, BLK)) for c in range(dc // BLK)],
                axis=1,
            )

        def pick(value, slot):
            got = value[:, slot * rpd : (slot + 1) * rpd]
            for i in range(1, nt2):
                at = (2 * i + slot) * rpd
                got = jnp.where(mine == i, value[:, at : at + rpd], got)
            return got

        for slot in range(2):
            gp[slot] = pick(gain_c[...], slot)
        for k in range(1, nt2):
            frm = lax.rem(mine + nt2 - k, nt2)
            recv(sc_hbm, sc_all.at[frm], sc_sem.at[k])
        for ti in range(nt2):
            for slot in range(2):
                power = jnp.exp2(sc_all[ti, (tp0 + slot) * rpd // BLK].astype(F32))
                scs[ti, slot] = jnp.concatenate(
                    [jnp.broadcast_to(power[:, c : c + 1], (2, BLK)) for c in range(lc // BLK)],
                    axis=1,
                )
        for k in range(1, ndp):
            frm = lax.rem(dp + ndp - k, ndp)
            recv(hrecv.at[frm], hrecv.at[frm], h_sem.at[k])
        for s in range(steps):
            x = jnp.concatenate([hrecv[d, s].astype(F32) for d in range(ndp)], axis=0)
            for slot in range(2):
                hp[s, slot] = pick(x, slot)

        lane = lax.broadcasted_iota(jnp.int32, (rows, LANES), 1)

        def placer(width):
            row = lax.broadcasted_iota(jnp.int32, (width, 4 * width), 0)
            col = lax.broadcasted_iota(jnp.int32, (width, 4 * width), 1)
            want = jnp.where(col < 2 * width, 2 * row, 2 * row + 1 + 2 * width)
            return (col == want).astype(BF16)

        def spread(y, place):
            width = place.shape[0]
            n, count = y.shape[0], y.shape[1] // width
            if count > 1:
                y = jnp.concatenate(
                    [y[:, i * width : (i + 1) * width] for i in range(count)], axis=0
                )
            wide = jnp.dot(y, place, preferred_element_type=F32).astype(BF16)
            halves = [
                jnp.concatenate(
                    [
                        wide[i * n : (i + 1) * n, h * 2 * width : (h + 1) * 2 * width]
                        for i in range(count)
                    ],
                    axis=1,
                )
                for h in range(2)
            ]
            return jnp.concatenate(halves, axis=0)

        place_w = placer(LANES)
        place_c = place_w if rpd == LANES else placer(rpd)
        wr = wv.reshape(nchunk, 2 * dc, LANES)
        cvr = cv.reshape(nt2, 2, nchunk, 2 * rpd, LANES)
        skips = []
        for j in range(nchunk):
            v = jnp.zeros((rows, LANES), F32)
            for i in range(hpc):
                h = j * hpc + i
                inside = (lane >= i * psize) & (lane < (i + 1) * psize)
                v = jnp.where(inside, skip_ref[:, h : h + 1], v)
            skips.append(v)
        skip = jnp.concatenate(skips, axis=1)
        row_n = lax.broadcasted_iota(jnp.int32, (rows, nstate), 0)

        group = tp // gsz
        member = tp - group * gsz
        half_t = tp // nb
        idx_t = tp - half_t * nb
        to_group = idx_t // per
        slot_t = half_t * per + lax.rem(idx_t, per)
        flat = dp * ntp + tp
        last_owner = flat // ndp
        last_slot = lax.rem(flat, ndp)
        keep = jnp.ones((rows, lc), F32)
        added = []
        bmats = []
        for s in range(steps):
            if s > 0:
                recv(ags.at[0], agr.at[s - 1, sib], a_sem.at[s - 1, 1])
            spreads = []
            for slot in range(2):
                x = hp[s, slot]
                if s > 0:
                    x = x + jnp.concatenate(
                        [agr[s - 1, tp0 + slot, d].astype(F32) for d in range(ndp)], axis=0
                    )
                spreads.append(spread((x * gp[slot]).astype(BF16), place_c))
            width = min(256, lc)
            for k in list(range(1, nt2)) + [0]:
                ti = lax.rem(mine + k, nt2)
                if s == 0:
                    for ct in range(nchunk):
                        pltpu.make_async_copy(
                            codes_hbm.at[:, :, columns(ti, core, ct)], cv.at[ti, core, ct],
                            cl_sem.at[k, ct],
                        ).wait()
                        recv(
                            cv.at[ti, 1 - core, ct], cv.at[ti, 1 - core, ct], v_sem.at[k, ct]
                        )
                for c in range(0, lc, width):
                    parts = []
                    for slot in range(2):
                        w = jnp.concatenate(
                            [
                                cvr[ti, slot, ct]
                                for ct in range(c // LANES, (c + width) // LANES)
                            ],
                            axis=1,
                        )
                        p = jnp.dot(spreads[slot], w, preferred_element_type=F32)
                        parts.append(
                            [
                                p[h * allr : (h + 1) * allr]
                                * scs[ti, slot, h : h + 1, c : c + width]
                                for h in range(2)
                            ]
                        )
                    for h in range(2):
                        p = parts[0][h] + parts[1][h]
                        for d in range(ndp):
                            d1s[s, ti, d, :, h * lc + c : h * lc + c + width] = p[
                                d * rows : (d + 1) * rows
                            ].astype(BF16)
                for m in range(1, ndp):
                    peer = lax.rem(dp + m, ndp)
                    send(d1s.at[s, ti, peer], d1r.at[s, ti, m], d1_sem.at[s, ti, m], peer, tp)

            xo = hown[s].astype(F32)
            if s > 0:
                for k in range(2, ntp):
                    recv(ags.at[0], agr.at[s - 1, tp ^ k], a_sem.at[s - 1, k])
                for k in range(1, ndp):
                    frm = lax.rem(dp + ndp - k, ndp)
                    for m in range(ntp):
                        recv(xr.at[s - 1, frm, tp ^ m], xr.at[s - 1, frm, tp ^ m],
                             x_sem.at[s - 1, k, m])
                for t in range(ntp):
                    xr[s - 1, dp, t] = agr[s - 1, t, dp]
                xo = xo + jnp.concatenate(
                    [xr[s - 1, d, t].astype(F32) for d in range(ndp) for t in range(ntp)], axis=1
                )
            inv = lax.rsqrt(jnp.sum(xo * xo, axis=1, keepdims=True) / feats + EPS)
            yo = (xo * gain_ref[...]).astype(BF16)
            if s == 0:
                load_bc.wait()
            hb[s + 3] = jnp.dot(yo, wbc[...], preferred_element_type=F32) * inv
            mixed = convb_ref[4:5, :]
            for i in range(4):
                mixed = mixed + hb[s + i] * convb_ref[i : i + 1, :]
            piece = silu(mixed)
            cs[s] = piece
            for m in range(gsz):
                target = to_group * gsz + m

                @pl.when(target != tp)
                def _(s=s, target=target):
                    remote(
                        cs.at[s], cr.at[s, slot_t], c_sem.at[s, slot_t], dp, target
                    ).start()

                @pl.when(target == tp)
                def _(s=s, piece=piece):
                    cr[s, slot_t] = piece

            x = jnp.concatenate([hrecv[d, s].astype(F32) for d in range(ndp)], axis=0)
            if s > 0:
                x = x + jnp.concatenate(
                    [
                        jnp.concatenate(
                            [agr[s - 1, t, d].astype(F32) for d in range(ndp)], axis=0
                        )
                        for t in range(ntp)
                    ],
                    axis=1,
                )
            wide = spread((x * gain_c[...]).astype(BF16), place_w)
            if s == 0:
                for copy in load_w:
                    copy.wait()
            for c in range(0, lc, width):
                w = jnp.concatenate(
                    [wr[ct] for ct in range(c // LANES, (c + width) // LANES)], axis=1
                )
                p = jnp.dot(wide, w, preferred_element_type=F32)
                for h in range(2):
                    for d in range(ndp):
                        s2[s, d, :, h * lc + c : h * lc + c + width] = p[
                            h * allr + d * rows : h * allr + (d + 1) * rows
                        ].astype(BF16)
            for k in range(1, ndp):
                peer = lax.rem(dp + k, ndp)
                send(s2.at[s, peer], r2.at[s, k], sem2.at[s, k], peer, tp)

            z = lax.dot_general(
                yo, wdt_ref[...], (((1,), (1,)), ((), ())), preferred_element_type=F32
            )
            z = z[:, :heads] * inv + dtb_ref[...]
            dt = jnp.maximum(z, 0.0) + jnp.log1p(jnp.exp(-jnp.abs(z)))
            decay = jnp.exp(-dt * rate_ref[...])

            delta = None
            for k in list(range(1, nt2)) + [0]:
                ti = lax.rem(mine + k, nt2)
                total = d1s[s, ti, dp].astype(F32)
                for m in range(1, ndp):
                    recv(d1s.at[s, ti, 0], d1r.at[s, ti, m], d1_sem.at[s, ti, m])
                    total = total + d1r[s, ti, m].astype(F32)
                if k > 0:
                    d2s[s, k] = total.astype(BF16)
                    send(d2s.at[s, k], d2r.at[s, k], d2_sem.at[s, k], dp, 2 * ti + core)
                else:
                    delta = total

            if s == 0:
                load_out.wait()
                load_oc.wait()

                @pl.loop(0, lc // 32)
                def _(i):
                    at = pl.ds(pl.multiple_of(i * 32, 32), 32)
                    change = ocodes_ref[at, :].astype(F32) * so_ref[i // (BLK // 32)]
                    wo[at, :] = (wo[at, :].astype(F32) + change).astype(BF16)

                for r in range(rows):
                    load_st[r].wait()

                    @pl.loop(0, nchunk)
                    def _(j, r=r):
                        at = pl.ds(pl.multiple_of(j * LANES, LANES), LANES)
                        sb[at, r * nstate : (r + 1) * nstate] = state[r, at].astype(BF16)

            for q in range(2 * per):
                frm = (q // per) * nb + group * per + q % per

                @pl.when(frm != tp)
                def _(s=s, q=q):
                    recv(cs.at[s], cr.at[s, q], c_sem.at[s, q])

            bmat = [cr[s, i] for i in range(per)]
            cmat = [cr[s, per + i] for i in range(per)]
            bmat = bmat[0] if per == 1 else jnp.concatenate(bmat, axis=1)
            cmat = cmat[0] if per == 1 else jnp.concatenate(cmat, axis=1)
            bst_ref[s] = bmat
            bmats.append(bmat)
            high = cmat.astype(BF16).astype(F32)
            low = cmat - high
            query = jnp.concatenate(
                [
                    jnp.concatenate(
                        [jnp.where(row_n == r, v, 0.0) for r in range(rows)], axis=1
                    )
                    for v in (high, low)
                ],
                axis=0,
            ).astype(BF16)
            reads = []
            for c in range(0, lc, width):
                q = lax.dot_general(
                    query, sb[c : c + width, :], (((1,), (1,)), ((), ())),
                    preferred_element_type=F32,
                )
                reads.append(q[:rows] + q[rows:])
            reads = jnp.concatenate(reads, axis=1)

            total = delta + s2[s, dp].astype(F32)
            for k in range(1, ndp):
                recv(s2.at[s, 0], r2.at[s, k], sem2.at[s, k])
                total = total + r2[s, k].astype(F32)
            for k in range(1, nt2):
                recv(d2s.at[s, 0], d2r.at[s, k], d2_sem.at[s, k])
                total = total + d2r[s, k].astype(F32)
            hx[s + 3] = total[:, lc:] * inv
            mixed = convx_ref[4:5, :]
            for i in range(4):
                mixed = mixed + hx[s + i] * convx_ref[i : i + 1, :]
            inner = silu(mixed)
            dte, dece = [], []
            for j in range(nchunk):
                a = jnp.zeros((rows, LANES), F32)
                b = jnp.zeros((rows, LANES), F32)
                for i in range(hpc):
                    h = j * hpc + i
                    inside = (lane >= i * psize) & (lane < (i + 1) * psize)
                    a = jnp.where(inside, dt[:, h : h + 1], a)
                    b = jnp.where(inside, decay[:, h : h + 1], b)
                dte.append(a)
                dece.append(b)
            dte = jnp.concatenate(dte, axis=1)
            dece = jnp.concatenate(dece, axis=1)
            keep = keep * dece
            added = [v * dece for v in added] + [dte * inner]
            read = keep * reads + skip * inner
            for v, b in zip(added, bmats):
                read = read + v * jnp.sum(b * cmat, axis=1, keepdims=True)
            gated = read * silu(total[:, :lc] * inv)
            qs[s] = jnp.broadcast_to(
                jnp.sum(gated * gated, axis=1, keepdims=True), (rows, LANES)
            )
            gs[s] = (gated * ng_ref[...]).astype(BF16)
            gr[s, dp] = gs[s]
            qr[s, dp, member] = qs[s]
            for k in range(1, ndp):
                send(gs.at[s], gr.at[s, dp], g_sem.at[s, k], lax.rem(dp + k, ndp), tp)
            for k in range(ndp):
                for m in range(gsz):
                    if k + m > 0:
                        send(
                            qs.at[s], qr.at[s, dp, member], q_sem.at[s, k, m],
                            lax.rem(dp + k, ndp), group * gsz + lax.rem(member + m, gsz),
                        )
            if s == steps - 1:
                for j in range(nchunk):
                    here = slice(j * LANES, (j + 1) * LANES)
                    coef_ref[j] = jnp.concatenate(
                        [keep[:, here]] + [v[:, here] for v in added], axis=0
                    )
            for k in range(ndp):
                frm_d = lax.rem(dp + ndp - k, ndp)
                if k > 0:
                    recv(gs.at[s], gr.at[s, frm_d], g_sem.at[s, k])
                for m in range(gsz):
                    if k + m > 0:
                        frm = lax.rem(member + gsz - m, gsz)
                        recv(qs.at[s], qr.at[s, frm_d, frm], q_sem.at[s, k, m])
            every = jnp.concatenate(
                [gr[s, d].astype(F32) for d in range(ndp)], axis=0
            ).astype(BF16)
            scales = []
            for d in range(ndp):
                sq = qr[s, d, 0]
                for m in range(1, gsz):
                    sq = sq + qr[s, d, m]
                scales.append(lax.rsqrt(sq[:, :1] / (di // G) + EPS))
            scale = jnp.concatenate(scales, axis=0)
            wide_o = max(ac, min(256, dc))
            for c in range(0, dc, wide_o):
                p = jnp.dot(every, wo[:, c : c + wide_o], preferred_element_type=F32) * scale
                for i in range(wide_o // ac):
                    os[s, c // ac + i] = p[:, i * ac : (i + 1) * ac].astype(BF16)
            for k in range(1, ntp):
                peer = tp ^ k
                send(os.at[s, peer], orv.at[s, k], o_sem.at[s, k], dp, peer)
            total = os[s, tp].astype(F32)
            for k in range(1, ntp):
                recv(os.at[s, 0], orv.at[s, k], o_sem.at[s, k])
                total = total + orv[s, k].astype(F32)
            for d in range(ndp):
                ags[s, d] = total[d * rows : (d + 1) * rows].astype(BF16)
            if s < steps - 1:
                for k in range(1, ntp):
                    send(ags.at[s], agr.at[s, tp], a_sem.at[s, k], dp, tp ^ k)
                for k in range(1, ndp):
                    peer = lax.rem(dp + k, ndp)
                    for m in range(ntp):
                        send(
                            ags.at[s, peer], xr.at[s, dp, tp], x_sem.at[s, k, m], peer, tp ^ m
                        )
                agr[s, tp] = ags[s]

        def final(d):
            return remote(
                ags.at[steps - 1, d], mr.at[last_slot], f_sem.at[last_slot], d, last_owner
            )

        for k in range(ndp):
            d = lax.rem(dp + k, ndp)
            if k > 0:
                final(d).start()
            else:

                @pl.when(last_owner != tp)
                def _():
                    final(d).start()

                @pl.when(last_owner == tp)
                def _():
                    mr[last_slot] = ags[steps - 1, dp]

        sources = [tp * ndp + i for i in range(ndp)]
        for s in range(steps - 1):
            out_ref[s] = jnp.concatenate(
                [xr[s, f // ntp, lax.rem(f, ntp)].astype(F32) for f in sources], axis=1
            ).astype(BF16)
        for i, f in enumerate(sources):

            @pl.when(f != flat)
            def _(i=i):
                recv(mr.at[i], mr.at[i], f_sem.at[i])

        out_ref[steps - 1] = jnp.concatenate(
            [mr[i].astype(F32) for i in range(ndp)], axis=1
        ).astype(BF16)

        for copy in pending:
            copy.wait_send()
        for s in range(steps):
            for m in range(gsz):
                target = to_group * gsz + m

                @pl.when(target != tp)
                def _(s=s, target=target):
                    remote(
                        cs.at[s], cr.at[s, slot_t], c_sem.at[s, slot_t], dp, target
                    ).wait_send()

        for k in range(ndp):
            d = lax.rem(dp + k, ndp)
            if k > 0:
                final(d).wait_send()
            else:

                @pl.when(last_owner != tp)
                def _():
                    final(d).wait_send()

    vm = pltpu.VMEM
    dma = pltpu.SemaphoreType.DMA
    scratch = [
        vm((rows, lc, nstate), F32),
        vm((lc, rows * nstate), BF16),
        vm((steps + 3, rows, lc), F32),
        vm((steps + 3, rows, cb), F32),
        vm((steps, rows, feats), BF16),
        vm((ndp, steps, rows, dc), BF16),
        vm((steps, 2, allr, rpd), F32),
        vm((2, 1, rpd), F32),
        vm((steps, nt2, ndp, rows, 2 * lc), BF16),
        vm((steps, nt2, ndp, rows, 2 * lc), BF16),
        vm((steps, nt2, rows, 2 * lc), BF16),
        vm((steps, nt2, rows, 2 * lc), BF16),
        vm((steps, ndp, rows, 2 * lc), BF16),
        vm((steps, ndp, rows, 2 * lc), BF16),
        vm((steps, rows, cb), F32),
        vm((steps, 2 * per, rows, cb), F32),
        vm((steps, rows, lc), BF16),
        vm((steps, ndp, rows, lc), BF16),
        vm((steps, rows, LANES), F32),
        vm((steps, ndp, gsz, rows, LANES), F32),
        vm((steps, ntp, allr, ac), BF16),
        vm((steps, ntp, allr, ac), BF16),
        vm((steps, ndp, rows, ac), BF16),
        vm((steps, ntp, ndp, rows, ac), BF16),
        vm((steps, ndp, ntp, rows, ac), BF16),
        vm((ndp, rows, ac), BF16),
        vm((nt2, 2, nchunk, rpd, 2, LANES), BF16),
        vm((nchunk, dc, 2, LANES), BF16),
        vm((feats, cb), BF16),
        vm((lc, dc), BF16),
        vm((nt2, nkb, 2, lc // BLK), jnp.int32),
        vm((nt2, 2, 2, lc), F32),
        vm((1, feats), F32),
        vm((1, dc), F32),
        vm((heads, feats), BF16),
        vm((LANES, feats), BF16),
        vm((lc // BLK, 1, dc // BLK), jnp.int32),
        vm((lc // BLK, 1, dc), F32),
        vm((lc, dc), BF16),
        vm((5, lc), F32),
        vm((5, cb), F32),
        vm((1, heads), F32),
        vm((1, heads), F32),
        vm((1, heads), F32),
        vm((1, lc), F32),
        vm((3, rows, lc), BF16),
        vm((3, rows, cb), BF16),
        dma((15,)),
        dma((3 + nchunk,)),
        dma((nt2, nchunk)),
        dma((rows,)),
        dma(()),
        dma((nt2, nchunk)),
        dma((nt2,)),
        dma((ndp,)),
        dma((steps, nt2, ndp)),
        dma((steps, nt2)),
        dma((steps, ndp)),
        dma((steps, 2 * per)),
        dma((steps, ndp)),
        dma((steps, ndp, gsz)),
        dma((steps, ntp)),
        dma((steps, ntp)),
        dma((steps, ndp, ntp)),
        dma((ndp,)),
    ]
    vspec = pl.BlockSpec(memory_space=pltpu.VMEM)
    hspec = pl.BlockSpec(memory_space=pl.ANY)
    return pl.pallas_call(
        kernel,
        out_shape=(
            jax.ShapeDtypeStruct((steps, rows, oc), BF16),
            jax.ShapeDtypeStruct((nchunk, (1 + steps) * rows, LANES), F32),
            jax.ShapeDtypeStruct((steps, rows, nstate), F32),
        ),
        in_specs=[hspec] * 19,
        out_specs=(vspec, vspec, vspec),
        scratch_shapes=scratch,
        compiler_params=pltpu.CompilerParams(
            collective_id=0, has_side_effects=True, vmem_limit_bytes=60 * 1024 * 1024
        ),
    )


def make_update(steps, rows, nchunk, nstate, oc):
    count = steps * rows
    depth = -(-(rows + 3 * count) // LANES) * LANES

    def kernel(state_ref, coef_ref, bst_ref, mixed_ref, new_ref, out_ref, rhs):
        @pl.when(pl.program_id(0) == 0)
        def _():
            out_ref[...] = mixed_ref[...]
            b = jnp.concatenate([bst_ref[s] for s in range(steps)], axis=0)
            row = lax.rem(lax.broadcasted_iota(jnp.int32, (count, nstate), 0), rows)
            for r in range(rows):
                v = jnp.where(row == r, b, 0.0)
                high = v.astype(BF16).astype(F32)
                rhs[:, r * nstate : (r + 1) * nstate] = jnp.concatenate(
                    [
                        jnp.zeros((rows, nstate), F32), high, high, v - high,
                        jnp.zeros((depth - rows - 3 * count, nstate), F32),
                    ],
                    axis=0,
                ).astype(BF16)

        keep = coef_ref[0, :rows]
        added = coef_ref[0, rows:]
        high = added.astype(BF16).astype(F32)
        full = jnp.concatenate(
            [keep, high, added - high, high, jnp.zeros((depth - rows - 3 * count, LANES), F32)],
            axis=0,
        ).T
        lhs = full.astype(BF16)
        for r in range(rows):
            u = jnp.dot(
                lhs, rhs[:, r * nstate : (r + 1) * nstate], preferred_element_type=F32
            )
            new_ref[r, 0] = full[:, r : r + 1] * state_ref[r, 0] + u

    block = pl.BlockSpec((rows, 1, LANES, nstate), lambda j: (0, j, 0, 0))
    return pl.pallas_call(
        kernel,
        grid=(nchunk,),
        out_shape=(
            jax.ShapeDtypeStruct((rows, nchunk, LANES, nstate), F32),
            jax.ShapeDtypeStruct((steps, rows, oc), BF16),
        ),
        in_specs=[
            block,
            pl.BlockSpec((1, (1 + steps) * rows, LANES), lambda j: (j, 0, 0)),
            pl.BlockSpec((steps, rows, nstate), lambda j: (0, 0, 0)),
            pl.BlockSpec((steps, rows, oc), lambda j: (0, 0, 0)),
        ],
        out_specs=(block, pl.BlockSpec((steps, rows, oc), lambda j: (0, 0, 0))),
        scratch_shapes=[pltpu.VMEM((depth, rows * nstate), BF16)],
        compiler_params=pltpu.CompilerParams(vmem_limit_bytes=32 * 1024 * 1024),
    )


def body(
    hidden_in, pre_gain, w_zx, zx_codes, zx_exponents, w_bc, w_dt, conv_x, conv_bc, dt_bias,
    decay_rate, skip_gain, conv_state_x, conv_state_bc, ssm_state, norm_gain, w_out, out_codes,
    out_exponents,
):
    ndp, ntp = lax.axis_size("dp"), lax.axis_size("tp")
    steps, rows, feats = hidden_in.shape
    dc = feats // ndp
    lc = w_zx.shape[2]
    cb = w_bc.shape[1]
    _, heads, psize, nstate = ssm_state.shape
    gsz = ntp // G
    di = lc * ntp

    call = make_kernel(ndp, ntp, steps, rows, dc, lc, cb, heads, psize, nstate, gsz, feats, di)
    mixed, coef, bst = call(
        hidden_in, pre_gain[None], w_dt.T, zx_exponents, out_exponents[:, None], out_codes, conv_x,
        conv_bc, dt_bias[None], decay_rate[None], skip_gain[None], norm_gain[None],
        conv_state_x.transpose(1, 0, 2), conv_state_bc.transpose(1, 0, 2),
        ssm_state.reshape(rows, lc, nstate),
        zx_codes, w_zx, w_bc, w_out,
    )
    update = make_update(steps, rows, lc // LANES, nstate, feats // ntp)
    state, out = update(
        ssm_state.reshape(rows, lc // LANES, LANES, nstate), coef, bst, mixed
    )
    return out, state.reshape(ssm_state.shape)


def solution(mesh):
    return jax.shard_map(
        body,
        mesh=mesh,
        in_specs=(
            P(None, "dp", None),
            P(),
            P(None, None, "tp"),
            P(("dp", "tp"), None, None),
            P("dp", None, "tp"),
            P(None, "tp"),
            P(None, "tp"),
            P(None, "tp"),
            P(None, "tp"),
            P("tp"),
            P("tp"),
            P("tp"),
            P("dp", None, "tp"),
            P("dp", None, "tp"),
            P("dp", "tp", None, None),
            P("tp"),
            P("tp", None),
            P("tp", "dp"),
            P("tp", "dp"),
        ),
        out_specs=(P(None, "dp", "tp"), P("dp", "tp", None, None)),
        check_vma=False,
    )
```

```python
import jax
import jax.numpy as jnp
from jax import lax
from jax.experimental import pallas as pl
from jax.experimental.pallas import tpu as pltpu
from jax.sharding import PartitionSpec as P

G = 4
BLK = 128
LANES = 128
EPS = 1e-05
MESH = pl.DeviceIdType.MESH
F32 = jnp.float32
BF16 = jnp.bfloat16


def silu(v):
    return v / (1.0 + jnp.exp(-v))


def make_kernel(ndp, ntp, steps, rows, dc, lc, cb, heads, psize, nstate, gsz, feats, di):
    oc = feats // ntp
    ac = dc // ntp
    nchunk = lc // LANES
    hpc = LANES // psize
    rpd = dc // ntp
    nt2 = ntp // 2
    nb = G * nstate // cb
    per = nstate // cb
    allr = ndp * rows
    nkb = dc // BLK

    def kernel(
        hid_hbm, gain_hbm, wdt_hbm, sc_hbm, so_hbm, ocodes_hbm, convx_hbm, convb_hbm, dtb_hbm,
        rate_hbm, skip_hbm, ng_hbm, hx0_hbm, hb0_hbm, state_hbm, codes_hbm, wzx_hbm, wbc_hbm,
        wout_hbm,
        out_ref, coef_ref, bst_ref,
        state, sb, hx, hb, hown, hrecv, hp, gp, d1s, d1r, d2s, d2r, s2, r2, cs, cr, gs, gr, qs, qr,
        os, orv, ags, agr, xr, mr,
        cv, wv, wbc, wo, sc_all, scs,
        gain_ref, gain_c, wdt_in, wdt_ref, so_in, so_ref, ocodes_ref, convx_ref, convb_ref,
        dtb_ref, rate_ref, skip_ref, ng_ref, hx0_ref, hb0_ref,
        l_sems, w_sems, cl_sem, st_sem, send_sem, v_sem, sc_sem, h_sem, d1_sem, d2_sem, sem2, c_sem,
        g_sem, q_sem, o_sem, a_sem, x_sem, f_sem,
    ):
        dp = lax.axis_index("dp")
        tp = lax.axis_index("tp")
        core = lax.rem(tp, 2)
        tp0 = tp - core
        mine = tp // 2
        sib = tp ^ 1
        group = tp // gsz
        member = tp - group * gsz
        half_t = tp // nb
        idx_t = tp - half_t * nb
        to_group = idx_t // per
        slot_t = half_t * per + lax.rem(idx_t, per)
        flat = dp * ntp + tp
        last_owner = flat // ndp
        last_slot = lax.rem(flat, ndp)
        sources = [tp * ndp + i for i in range(ndp)]
        pending = []

        def remote(src, dst, rsem, d, t):
            return pltpu.make_async_remote_copy(
                src_ref=src, dst_ref=dst, send_sem=send_sem, recv_sem=rsem,
                device_id=(d, t), device_id_type=MESH,
            )

        def send(src, dst, rsem, d, t):
            copy = remote(src, dst, rsem, d, t)
            copy.start()
            pending.append(copy)

        def recv(src, dst, rsem):
            remote(src, dst, rsem, dp, tp).wait_recv()

        def chunk(i):
            return pl.ds(pl.multiple_of(i * dc, LANES), dc)

        def columns(ti, par, ct):
            return pl.ds(pl.multiple_of((2 * ti + par) * lc + ct * LANES, LANES), LANES)

        small_loads = [
            (hid_hbm, hown), (hid_hbm.at[:, :, chunk(dp)], hrecv.at[dp]),
            (gain_hbm, gain_ref), (gain_hbm.at[:, chunk(dp)], gain_c),
            (sc_hbm, sc_all.at[mine]), (wdt_hbm, wdt_in), (so_hbm, so_in),
            (convx_hbm, convx_ref), (convb_hbm, convb_ref), (dtb_hbm, dtb_ref),
            (rate_hbm, rate_ref), (skip_hbm, skip_ref), (ng_hbm, ng_ref), (hx0_hbm, hx0_ref),
            (hb0_hbm, hb0_ref),
        ]
        small_loads = [
            pltpu.make_async_copy(a, b, l_sems.at[i]) for i, (a, b) in enumerate(small_loads)
        ]
        for copy in small_loads:
            copy.start()
        own_codes = []
        for k in list(range(1, nt2)) + [0]:
            ti = lax.rem(mine + k, nt2)
            for ct in range(nchunk):
                copy = pltpu.make_async_copy(
                    codes_hbm.at[:, :, columns(ti, core, ct)], cv.at[ti, core, ct],
                    cl_sem.at[k, ct],
                )
                copy.start()
                own_codes.append(copy)
        load_bc = pltpu.make_async_copy(wbc_hbm, wbc, w_sems.at[0])
        load_bc.start()

        barrier = pltpu.get_barrier_semaphore()

        def greet(d, t):
            pl.semaphore_signal(barrier, inc=1, device_id=(d, t), device_id_type=MESH)

        greeted = ntp - 1 + (ndp - 1) * gsz
        for k in range(1, ndp):
            for m in range(gsz):
                greet(lax.rem(dp + k, ndp), group * gsz + lax.rem(member + m, gsz))
        for k in range(1, ntp):
            greet(dp, tp ^ k)
        for f in sources:

            @pl.when(f != flat)
            def _(f=f):
                greet(f // ntp, lax.rem(f, ntp))

        @pl.when(last_owner == tp)
        def _():
            pl.semaphore_wait(barrier, greeted + ndp - 1)

        @pl.when(last_owner != tp)
        def _():
            pl.semaphore_wait(barrier, greeted + ndp)

        for k in range(1, nt2):
            ti = lax.rem(mine + k, nt2)
            send(sc_hbm, sc_all.at[mine], sc_sem.at[k], dp, 2 * ti + core)
        for k in range(1, ndp):
            peer = lax.rem(dp + k, ndp)
            send(hid_hbm.at[:, :, chunk(peer)], hrecv.at[dp], h_sem.at[k], peer, tp)
        for k in list(range(1, nt2)) + [0]:
            ti = lax.rem(mine + k, nt2)
            for ct in range(nchunk):
                send(
                    codes_hbm.at[:, :, columns(ti, 1 - core, ct)], cv.at[ti, core, ct],
                    v_sem.at[k, ct], dp, sib,
                )
        load_w = []
        for ct in range(nchunk):
            copy = pltpu.make_async_copy(
                wzx_hbm.at[pl.ds(dp * dc, dc), :, pl.ds(ct * LANES, LANES)], wv.at[ct],
                w_sems.at[1 + ct],
            )
            copy.start()
            load_w.append(copy)
        load_st = []
        for r in range(rows):
            copy = pltpu.make_async_copy(state_hbm.at[r], state.at[r], st_sem.at[r])
            copy.start()
            load_st.append(copy)
        load_out = pltpu.make_async_copy(
            wout_hbm.at[:, pl.ds(pl.multiple_of(dp * dc, LANES), dc)], wo, w_sems.at[1 + nchunk]
        )
        load_out.start()
        load_oc = pltpu.make_async_copy(ocodes_hbm, ocodes_ref, w_sems.at[2 + nchunk])
        load_oc.start()

        for copy in small_loads:
            copy.wait()
        wdt_ref[...] = jnp.concatenate(
            [wdt_in[...].astype(F32), jnp.zeros((LANES - heads, feats), F32)], axis=0
        ).astype(BF16)
        hx[0:3] = hx0_ref[...].astype(F32)
        hb[0:3] = hb0_ref[...].astype(F32)
        power = jnp.exp2(so_in[...].astype(F32))
        for b in range(lc // BLK):
            so_ref[b] = jnp.concatenate(
                [jnp.broadcast_to(power[b, :, c : c + 1], (1, BLK)) for c in range(dc // BLK)],
                axis=1,
            )

        def pick(value, slot):
            got = value[:, slot * rpd : (slot + 1) * rpd]
            for i in range(1, nt2):
                at = (2 * i + slot) * rpd
                got = jnp.where(mine == i, value[:, at : at + rpd], got)
            return got

        for slot in range(2):
            gp[slot] = pick(gain_c[...], slot)
        for k in range(1, nt2):
            frm = lax.rem(mine + nt2 - k, nt2)
            recv(sc_hbm, sc_all.at[frm], sc_sem.at[k])
        for ti in range(nt2):
            for slot in range(2):
                power = jnp.exp2(sc_all[ti, (tp0 + slot) * rpd // BLK].astype(F32))
                scs[ti, slot] = jnp.concatenate(
                    [jnp.broadcast_to(power[:, c : c + 1], (2, BLK)) for c in range(lc // BLK)],
                    axis=1,
                )
        for k in range(1, ndp):
            frm = lax.rem(dp + ndp - k, ndp)
            recv(hrecv.at[frm], hrecv.at[frm], h_sem.at[k])
        for s in range(steps):
            x = jnp.concatenate([hrecv[d, s].astype(F32) for d in range(ndp)], axis=0)
            for slot in range(2):
                hp[s, slot] = pick(x, slot)

        lane = lax.broadcasted_iota(jnp.int32, (rows, LANES), 1)

        def placer(width):
            row = lax.broadcasted_iota(jnp.int32, (width, 4 * width), 0)
            col = lax.broadcasted_iota(jnp.int32, (width, 4 * width), 1)
            want = jnp.where(col < 2 * width, 2 * row, 2 * row + 1 + 2 * width)
            return (col == want).astype(BF16)

        def spread(y, place):
            width = place.shape[0]
            n, count = y.shape[0], y.shape[1] // width
            if count > 1:
                y = jnp.concatenate(
                    [y[:, i * width : (i + 1) * width] for i in range(count)], axis=0
                )
            wide = jnp.dot(y, place, preferred_element_type=F32).astype(BF16)
            halves = [
                jnp.concatenate(
                    [
                        wide[i * n : (i + 1) * n, h * 2 * width : (h + 1) * 2 * width]
                        for i in range(count)
                    ],
                    axis=1,
                )
                for h in range(2)
            ]
            return jnp.concatenate(halves, axis=0)

        place_w = placer(LANES)
        place_c = place_w if rpd == LANES else placer(rpd)
        wr = wv.reshape(nchunk, 2 * dc, LANES)
        cvr = cv.reshape(nt2, 2, nchunk, 2 * rpd, LANES)
        skips = []
        for j in range(nchunk):
            v = jnp.zeros((rows, LANES), F32)
            for i in range(hpc):
                h = j * hpc + i
                inside = (lane >= i * psize) & (lane < (i + 1) * psize)
                v = jnp.where(inside, skip_ref[:, h : h + 1], v)
            skips.append(v)
        skip = jnp.concatenate(skips, axis=1)
        row_n = lax.broadcasted_iota(jnp.int32, (rows, nstate), 0)

        keep = jnp.ones((rows, lc), F32)
        added = []
        bmats = []
        for s in range(steps):
            if s > 0:
                recv(ags.at[0], agr.at[s - 1, sib], a_sem.at[s - 1, 1])
            spreads = []
            for slot in range(2):
                x = hp[s, slot]
                if s > 0:
                    x = x + jnp.concatenate(
                        [agr[s - 1, tp0 + slot, d].astype(F32) for d in range(ndp)], axis=0
                    )
                spreads.append(spread((x * gp[slot]).astype(BF16), place_c))
            width = min(256, lc)
            for k in list(range(1, nt2)) + [0]:
                ti = lax.rem(mine + k, nt2)
                if s == 0:
                    for ct in range(nchunk):
                        pltpu.make_async_copy(
                            codes_hbm.at[:, :, columns(ti, core, ct)], cv.at[ti, core, ct],
                            cl_sem.at[k, ct],
                        ).wait()
                        recv(
                            cv.at[ti, 1 - core, ct], cv.at[ti, 1 - core, ct], v_sem.at[k, ct]
                        )
                for c in range(0, lc, width):
                    parts = []
                    for slot in range(2):
                        w = jnp.concatenate(
                            [
                                cvr[ti, slot, ct]
                                for ct in range(c // LANES, (c + width) // LANES)
                            ],
                            axis=1,
                        )
                        p = jnp.dot(spreads[slot], w, preferred_element_type=F32)
                        parts.append(
                            [
                                p[h * allr : (h + 1) * allr]
                                * scs[ti, slot, h : h + 1, c : c + width]
                                for h in range(2)
                            ]
                        )
                    for h in range(2):
                        p = parts[0][h] + parts[1][h]
                        for d in range(ndp):
                            d1s[s, ti, d, :, h * lc + c : h * lc + c + width] = p[
                                d * rows : (d + 1) * rows
                            ].astype(BF16)
                for m in range(1, ndp):
                    peer = lax.rem(dp + m, ndp)
                    send(d1s.at[s, ti, peer], d1r.at[s, ti, m], d1_sem.at[s, ti, m], peer, tp)

            if s > 0:
                for k in range(2, ntp):
                    recv(ags.at[0], agr.at[s - 1, tp ^ k], a_sem.at[s - 1, k])
            x = jnp.concatenate([hrecv[d, s].astype(F32) for d in range(ndp)], axis=0)
            if s > 0:
                x = x + jnp.concatenate(
                    [
                        jnp.concatenate(
                            [agr[s - 1, t, d].astype(F32) for d in range(ndp)], axis=0
                        )
                        for t in range(ntp)
                    ],
                    axis=1,
                )
            wide = spread((x * gain_c[...]).astype(BF16), place_w)
            if s == 0:
                for copy in load_w:
                    copy.wait()
            for c in range(0, lc, width):
                w = jnp.concatenate(
                    [wr[ct] for ct in range(c // LANES, (c + width) // LANES)], axis=1
                )
                p = jnp.dot(wide, w, preferred_element_type=F32)
                for h in range(2):
                    for d in range(ndp):
                        s2[s, d, :, h * lc + c : h * lc + c + width] = p[
                            h * allr + d * rows : h * allr + (d + 1) * rows
                        ].astype(BF16)
            for k in range(1, ndp):
                peer = lax.rem(dp + k, ndp)
                send(s2.at[s, peer], r2.at[s, k], sem2.at[s, k], peer, tp)

            xo = hown[s].astype(F32)
            if s > 0:
                for k in range(1, ndp):
                    frm = lax.rem(dp + ndp - k, ndp)
                    for m in range(ntp):
                        recv(xr.at[s - 1, frm, tp ^ m], xr.at[s - 1, frm, tp ^ m],
                             x_sem.at[s - 1, k, m])
                for t in range(ntp):
                    xr[s - 1, dp, t] = agr[s - 1, t, dp]
                xo = xo + jnp.concatenate(
                    [xr[s - 1, d, t].astype(F32) for d in range(ndp) for t in range(ntp)], axis=1
                )
            inv = lax.rsqrt(jnp.sum(xo * xo, axis=1, keepdims=True) / feats + EPS)
            yo = (xo * gain_ref[...]).astype(BF16)
            if s == 0:
                load_bc.wait()
            hb[s + 3] = jnp.dot(yo, wbc[...], preferred_element_type=F32) * inv
            mixed = convb_ref[4:5, :]
            for i in range(4):
                mixed = mixed + hb[s + i] * convb_ref[i : i + 1, :]
            piece = silu(mixed)
            cs[s] = piece
            for m in range(gsz):
                target = to_group * gsz + m

                @pl.when(target != tp)
                def _(s=s, target=target):
                    remote(
                        cs.at[s], cr.at[s, slot_t], c_sem.at[s, slot_t], dp, target
                    ).start()

                @pl.when(target == tp)
                def _(s=s, piece=piece):
                    cr[s, slot_t] = piece

            z = lax.dot_general(
                yo, wdt_ref[...], (((1,), (1,)), ((), ())), preferred_element_type=F32
            )
            z = z[:, :heads] * inv + dtb_ref[...]
            dt = jnp.maximum(z, 0.0) + jnp.log1p(jnp.exp(-jnp.abs(z)))
            decay = jnp.exp(-dt * rate_ref[...])

            delta = None
            for k in list(range(1, nt2)) + [0]:
                ti = lax.rem(mine + k, nt2)
                total = d1s[s, ti, dp].astype(F32)
                for m in range(1, ndp):
                    recv(d1s.at[s, ti, 0], d1r.at[s, ti, m], d1_sem.at[s, ti, m])
                    total = total + d1r[s, ti, m].astype(F32)
                if k > 0:
                    d2s[s, k] = total.astype(BF16)
                    send(d2s.at[s, k], d2r.at[s, k], d2_sem.at[s, k], dp, 2 * ti + core)
                else:
                    delta = total

            if s == 0:
                load_out.wait()
                load_oc.wait()

                @pl.loop(0, lc // 32)
                def _(i):
                    at = pl.ds(pl.multiple_of(i * 32, 32), 32)
                    change = ocodes_ref[at, :].astype(F32) * so_ref[i // (BLK // 32)]
                    wo[at, :] = (wo[at, :].astype(F32) + change).astype(BF16)

                for r in range(rows):
                    load_st[r].wait()

                    @pl.loop(0, nchunk)
                    def _(j, r=r):
                        at = pl.ds(pl.multiple_of(j * LANES, LANES), LANES)
                        sb[at, r * nstate : (r + 1) * nstate] = state[r, at].astype(BF16)

            for q in range(2 * per):
                frm = (q // per) * nb + group * per + q % per

                @pl.when(frm != tp)
                def _(s=s, q=q):
                    recv(cs.at[s], cr.at[s, q], c_sem.at[s, q])

            bmat = [cr[s, i] for i in range(per)]
            cmat = [cr[s, per + i] for i in range(per)]
            bmat = bmat[0] if per == 1 else jnp.concatenate(bmat, axis=1)
            cmat = cmat[0] if per == 1 else jnp.concatenate(cmat, axis=1)
            bst_ref[s] = bmat
            bmats.append(bmat)
            high = cmat.astype(BF16).astype(F32)
            low = cmat - high
            query = jnp.concatenate(
                [
                    jnp.concatenate(
                        [jnp.where(row_n == r, v, 0.0) for r in range(rows)], axis=1
                    )
                    for v in (high, low)
                ],
                axis=0,
            ).astype(BF16)
            reads = []
            for c in range(0, lc, width):
                q = lax.dot_general(
                    query, sb[c : c + width, :], (((1,), (1,)), ((), ())),
                    preferred_element_type=F32,
                )
                reads.append(q[:rows] + q[rows:])
            reads = jnp.concatenate(reads, axis=1)

            total = delta + s2[s, dp].astype(F32)
            for k in range(1, ndp):
                recv(s2.at[s, 0], r2.at[s, k], sem2.at[s, k])
                total = total + r2[s, k].astype(F32)
            for k in range(1, nt2):
                recv(d2s.at[s, 0], d2r.at[s, k], d2_sem.at[s, k])
                total = total + d2r[s, k].astype(F32)
            hx[s + 3] = total[:, lc:] * inv
            mixed = convx_ref[4:5, :]
            for i in range(4):
                mixed = mixed + hx[s + i] * convx_ref[i : i + 1, :]
            inner = silu(mixed)
            dte, dece = [], []
            for j in range(nchunk):
                a = jnp.zeros((rows, LANES), F32)
                b = jnp.zeros((rows, LANES), F32)
                for i in range(hpc):
                    h = j * hpc + i
                    inside = (lane >= i * psize) & (lane < (i + 1) * psize)
                    a = jnp.where(inside, dt[:, h : h + 1], a)
                    b = jnp.where(inside, decay[:, h : h + 1], b)
                dte.append(a)
                dece.append(b)
            dte = jnp.concatenate(dte, axis=1)
            dece = jnp.concatenate(dece, axis=1)
            keep = keep * dece
            added = [v * dece for v in added] + [dte * inner]
            read = keep * reads + skip * inner
            for v, b in zip(added, bmats):
                read = read + v * jnp.sum(b * cmat, axis=1, keepdims=True)
            gated = read * silu(total[:, :lc] * inv)
            square = jnp.broadcast_to(
                jnp.sum(gated * gated, axis=1, keepdims=True), (rows, LANES)
            )
            qs[s] = square
            high = square.astype(BF16)
            gs[s, :, :lc] = (gated * ng_ref[...]).astype(BF16)
            gs[s, :, lc : lc + LANES] = high
            gs[s, :, lc + LANES :] = (square - high.astype(F32)).astype(BF16)
            for k in range(1, ndp):
                send(gs.at[s], gr.at[s, dp], g_sem.at[s, k], lax.rem(dp + k, ndp), tp)
            for k in list(range(1, ndp)) + [0]:
                for m in range(1, gsz):
                    send(
                        qs.at[s], qr.at[s, dp, member], q_sem.at[s, k, m],
                        lax.rem(dp + k, ndp), group * gsz + lax.rem(member + m, gsz),
                    )
            gr[s, dp] = gs[s]
            if s == steps - 1:
                for j in range(nchunk):
                    here = slice(j * LANES, (j + 1) * LANES)
                    coef_ref[j] = jnp.concatenate(
                        [keep[:, here]] + [v[:, here] for v in added], axis=0
                    )
            for k in range(ndp):
                frm_d = lax.rem(dp + ndp - k, ndp)
                if k > 0:
                    recv(gs.at[s], gr.at[s, frm_d], g_sem.at[s, k])
                for m in range(1, gsz):
                    frm = lax.rem(member + gsz - m, gsz)
                    recv(qs.at[s], qr.at[s, frm_d, frm], q_sem.at[s, k, m])
            every = jnp.concatenate(
                [gr[s, d, :, :lc].astype(F32) for d in range(ndp)], axis=0
            ).astype(BF16)
            scales = []
            for d in range(ndp):
                sq = gr[s, d, :, lc : lc + LANES].astype(F32)
                sq = sq + gr[s, d, :, lc + LANES :].astype(F32)
                for m in range(1, gsz):
                    sq = sq + qr[s, d, lax.rem(member + m, gsz)]
                scales.append(lax.rsqrt(sq[:, :1] / (di // G) + EPS))
            scale = jnp.concatenate(scales, axis=0)
            wide_o = max(ac, min(256, dc))
            for c in range(0, dc, wide_o):
                p = jnp.dot(every, wo[:, c : c + wide_o], preferred_element_type=F32) * scale
                for i in range(wide_o // ac):
                    os[s, c // ac + i] = p[:, i * ac : (i + 1) * ac].astype(BF16)
            for k in range(1, ntp):
                peer = tp ^ k
                send(os.at[s, peer], orv.at[s, k], o_sem.at[s, k], dp, peer)
            total = os[s, tp].astype(F32)
            for k in range(1, ntp):
                recv(os.at[s, 0], orv.at[s, k], o_sem.at[s, k])
                total = total + orv[s, k].astype(F32)
            for d in range(ndp):
                ags[s, d] = total[d * rows : (d + 1) * rows].astype(BF16)
            if s < steps - 1:
                for k in range(1, ntp):
                    send(ags.at[s], agr.at[s, tp], a_sem.at[s, k], dp, tp ^ k)
                for k in range(1, ndp):
                    peer = lax.rem(dp + k, ndp)
                    for m in range(ntp):
                        send(
                            ags.at[s, peer], xr.at[s, dp, tp], x_sem.at[s, k, m], peer, tp ^ m
                        )
                agr[s, tp] = ags[s]

        def final(d):
            return remote(
                ags.at[steps - 1, d], mr.at[last_slot], f_sem.at[last_slot], d, last_owner
            )

        for k in range(ndp):
            d = lax.rem(dp + k, ndp)
            if k > 0:
                final(d).start()
            else:

                @pl.when(last_owner != tp)
                def _():
                    final(d).start()

                @pl.when(last_owner == tp)
                def _():
                    mr[last_slot] = ags[steps - 1, dp]

        for s in range(steps - 1):
            out_ref[s] = jnp.concatenate(
                [xr[s, f // ntp, lax.rem(f, ntp)].astype(F32) for f in sources], axis=1
            ).astype(BF16)
        for i, f in enumerate(sources):

            @pl.when(f != flat)
            def _(i=i):
                recv(mr.at[i], mr.at[i], f_sem.at[i])

        out_ref[steps - 1] = jnp.concatenate(
            [mr[i].astype(F32) for i in range(ndp)], axis=1
        ).astype(BF16)

        for copy in pending:
            copy.wait_send()
        for s in range(steps):
            for m in range(gsz):
                target = to_group * gsz + m

                @pl.when(target != tp)
                def _(s=s, target=target):
                    remote(
                        cs.at[s], cr.at[s, slot_t], c_sem.at[s, slot_t], dp, target
                    ).wait_send()

        for k in range(ndp):
            d = lax.rem(dp + k, ndp)
            if k > 0:
                final(d).wait_send()
            else:

                @pl.when(last_owner != tp)
                def _():
                    final(d).wait_send()

    vm = pltpu.VMEM
    dma = pltpu.SemaphoreType.DMA
    scratch = [
        vm((rows, lc, nstate), F32),
        vm((lc, rows * nstate), BF16),
        vm((steps + 3, rows, lc), F32),
        vm((steps + 3, rows, cb), F32),
        vm((steps, rows, feats), BF16),
        vm((ndp, steps, rows, dc), BF16),
        vm((steps, 2, allr, rpd), F32),
        vm((2, 1, rpd), F32),
        vm((steps, nt2, ndp, rows, 2 * lc), BF16),
        vm((steps, nt2, ndp, rows, 2 * lc), BF16),
        vm((steps, nt2, rows, 2 * lc), BF16),
        vm((steps, nt2, rows, 2 * lc), BF16),
        vm((steps, ndp, rows, 2 * lc), BF16),
        vm((steps, ndp, rows, 2 * lc), BF16),
        vm((steps, rows, cb), F32),
        vm((steps, 2 * per, rows, cb), F32),
        vm((steps, rows, lc + 2 * LANES), BF16),
        vm((steps, ndp, rows, lc + 2 * LANES), BF16),
        vm((steps, rows, LANES), F32),
        vm((steps, ndp, gsz, rows, LANES), F32),
        vm((steps, ntp, allr, ac), BF16),
        vm((steps, ntp, allr, ac), BF16),
        vm((steps, ndp, rows, ac), BF16),
        vm((steps, ntp, ndp, rows, ac), BF16),
        vm((steps, ndp, ntp, rows, ac), BF16),
        vm((ndp, rows, ac), BF16),
        vm((nt2, 2, nchunk, rpd, 2, LANES), BF16),
        vm((nchunk, dc, 2, LANES), BF16),
        vm((feats, cb), BF16),
        vm((lc, dc), BF16),
        vm((nt2, nkb, 2, lc // BLK), jnp.int32),
        vm((nt2, 2, 2, lc), F32),
        vm((1, feats), F32),
        vm((1, dc), F32),
        vm((heads, feats), BF16),
        vm((LANES, feats), BF16),
        vm((lc // BLK, 1, dc // BLK), jnp.int32),
        vm((lc // BLK, 1, dc), F32),
        vm((lc, dc), BF16),
        vm((5, lc), F32),
        vm((5, cb), F32),
        vm((1, heads), F32),
        vm((1, heads), F32),
        vm((1, heads), F32),
        vm((1, lc), F32),
        vm((3, rows, lc), BF16),
        vm((3, rows, cb), BF16),
        dma((15,)),
        dma((3 + nchunk,)),
        dma((nt2, nchunk)),
        dma((rows,)),
        dma(()),
        dma((nt2, nchunk)),
        dma((nt2,)),
        dma((ndp,)),
        dma((steps, nt2, ndp)),
        dma((steps, nt2)),
        dma((steps, ndp)),
        dma((steps, 2 * per)),
        dma((steps, ndp)),
        dma((steps, ndp, gsz)),
        dma((steps, ntp)),
        dma((steps, ntp)),
        dma((steps, ndp, ntp)),
        dma((ndp,)),
    ]
    vspec = pl.BlockSpec(memory_space=pltpu.VMEM)
    hspec = pl.BlockSpec(memory_space=pl.ANY)
    return pl.pallas_call(
        kernel,
        out_shape=(
            jax.ShapeDtypeStruct((steps, rows, oc), BF16),
            jax.ShapeDtypeStruct((nchunk, (1 + steps) * rows, LANES), F32),
            jax.ShapeDtypeStruct((steps, rows, nstate), F32),
        ),
        in_specs=[hspec] * 19,
        out_specs=(vspec, vspec, vspec),
        scratch_shapes=scratch,
        compiler_params=pltpu.CompilerParams(
            collective_id=0, has_side_effects=True, vmem_limit_bytes=60 * 1024 * 1024
        ),
    )


def make_update(steps, rows, nchunk, nstate, oc):
    count = steps * rows
    depth = -(-(rows + 3 * count) // LANES) * LANES
    rest = depth - rows - 3 * count

    def kernel(
        state_hbm, coef_hbm, bst_hbm, mixed_hbm, new_hbm, out_hbm,
        old, new, coef, bst, mixed, rhs, load_sem, store_sem, small_sem,
    ):
        small = [(coef_hbm, coef), (bst_hbm, bst), (mixed_hbm, mixed)]
        small = [
            pltpu.make_async_copy(a, b, small_sem.at[i]) for i, (a, b) in enumerate(small)
        ]
        for copy in small:
            copy.start()
        loads = [
            pltpu.make_async_copy(state_hbm.at[:, j], old.at[:, j], load_sem.at[j])
            for j in range(nchunk)
        ]
        for copy in loads:
            copy.start()
        for copy in small:
            copy.wait()
        stores = [pltpu.make_async_copy(mixed, out_hbm, small_sem.at[3])]
        stores[0].start()
        b = jnp.concatenate([bst[s] for s in range(steps)], axis=0)
        row = lax.rem(lax.broadcasted_iota(jnp.int32, (count, nstate), 0), rows)
        for r in range(rows):
            v = jnp.where(row == r, b, 0.0)
            high = v.astype(BF16).astype(F32)
            parts = [jnp.zeros((rows, nstate), F32), high, high, v - high]
            if rest:
                parts.append(jnp.zeros((rest, nstate), F32))
            rhs[:, r * nstate : (r + 1) * nstate] = jnp.concatenate(parts, axis=0).astype(BF16)
        for j in range(nchunk):
            keep = coef[j, :rows]
            added = coef[j, rows:]
            high = added.astype(BF16).astype(F32)
            parts = [keep, high, added - high, high]
            if rest:
                parts.append(jnp.zeros((rest, LANES), F32))
            full = jnp.concatenate(parts, axis=0).T
            lhs = full.astype(BF16)
            loads[j].wait()
            for r in range(rows):
                u = jnp.dot(
                    lhs, rhs[:, r * nstate : (r + 1) * nstate], preferred_element_type=F32
                )
                new[r, j] = full[:, r : r + 1] * old[r, j] + u
            copy = pltpu.make_async_copy(new.at[:, j], new_hbm.at[:, j], store_sem.at[j])
            copy.start()
            stores.append(copy)
        for copy in stores:
            copy.wait()

    vm = pltpu.VMEM
    hspec = pl.BlockSpec(memory_space=pl.ANY)
    return pl.pallas_call(
        kernel,
        out_shape=(
            jax.ShapeDtypeStruct((rows, nchunk, LANES, nstate), F32),
            jax.ShapeDtypeStruct((steps, rows, oc), BF16),
        ),
        in_specs=[hspec] * 4,
        out_specs=(hspec, hspec),
        scratch_shapes=[
            vm((rows, nchunk, LANES, nstate), F32),
            vm((rows, nchunk, LANES, nstate), F32),
            vm((nchunk, (1 + steps) * rows, LANES), F32),
            vm((steps, rows, nstate), F32),
            vm((steps, rows, oc), BF16),
            vm((depth, rows * nstate), BF16),
            pltpu.SemaphoreType.DMA((nchunk,)),
            pltpu.SemaphoreType.DMA((nchunk,)),
            pltpu.SemaphoreType.DMA((4,)),
        ],
        compiler_params=pltpu.CompilerParams(vmem_limit_bytes=60 * 1024 * 1024),
    )


def body(
    hidden_in, pre_gain, w_zx, zx_codes, zx_exponents, w_bc, w_dt, conv_x, conv_bc, dt_bias,
    decay_rate, skip_gain, conv_state_x, conv_state_bc, ssm_state, norm_gain, w_out, out_codes,
    out_exponents,
):
    ndp, ntp = lax.axis_size("dp"), lax.axis_size("tp")
    steps, rows, feats = hidden_in.shape
    dc = feats // ndp
    lc = w_zx.shape[2]
    cb = w_bc.shape[1]
    _, heads, psize, nstate = ssm_state.shape
    gsz = ntp // G
    di = lc * ntp

    call = make_kernel(ndp, ntp, steps, rows, dc, lc, cb, heads, psize, nstate, gsz, feats, di)
    mixed, coef, bst = call(
        hidden_in, pre_gain[None], w_dt.T, zx_exponents, out_exponents[:, None], out_codes, conv_x,
        conv_bc, dt_bias[None], decay_rate[None], skip_gain[None], norm_gain[None],
        conv_state_x.transpose(1, 0, 2), conv_state_bc.transpose(1, 0, 2),
        ssm_state.reshape(rows, lc, nstate),
        zx_codes, w_zx, w_bc, w_out,
    )
    update = make_update(steps, rows, lc // LANES, nstate, feats // ntp)
    state, out = update(
        ssm_state.reshape(rows, lc // LANES, LANES, nstate), coef, bst, mixed
    )
    return out, state.reshape(ssm_state.shape)


def solution(mesh):
    return jax.shard_map(
        body,
        mesh=mesh,
        in_specs=(
            P(None, "dp", None),
            P(),
            P(None, None, "tp"),
            P(("dp", "tp"), None, None),
            P("dp", None, "tp"),
            P(None, "tp"),
            P(None, "tp"),
            P(None, "tp"),
            P(None, "tp"),
            P("tp"),
            P("tp"),
            P("tp"),
            P("dp", None, "tp"),
            P("dp", None, "tp"),
            P("dp", "tp", None, None),
            P("tp"),
            P("tp", None),
            P("tp", "dp"),
            P("tp", "dp"),
        ),
        out_specs=(P(None, "dp", "tp"), P("dp", "tp", None, None)),
        check_vma=False,
    )
```

```python
import jax
import jax.numpy as jnp
from jax import lax
from jax.experimental import pallas as pl
from jax.experimental.pallas import tpu as pltpu
from jax.sharding import PartitionSpec as P

G = 4
BLK = 128
LANES = 128
EPS = 1e-05
MESH = pl.DeviceIdType.MESH
F32 = jnp.float32
BF16 = jnp.bfloat16


def silu(v):
    return v / (1.0 + jnp.exp(-v))


def make_kernel(ndp, ntp, steps, rows, dc, lc, cb, heads, psize, nstate, gsz, feats, di):
    oc = feats // ntp
    ac = dc // ntp
    nchunk = lc // LANES
    hpc = LANES // psize
    rpd = dc // ntp
    nt2 = ntp // 2
    nb = G * nstate // cb
    per = nstate // cb
    allr = ndp * rows
    nkb = dc // BLK

    def kernel(
        hid_hbm, gain_hbm, wdt_hbm, sc_hbm, so_hbm, ocodes_hbm, convx_hbm, convb_hbm, dtb_hbm,
        rate_hbm, skip_hbm, ng_hbm, hx0_hbm, hb0_hbm, state_hbm, codes_hbm, wzx_hbm, wbc_hbm,
        wout_hbm,
        out_ref, coef_ref, bst_ref,
        state, sb, hx, hb, hown, hrecv, hp, gp, d1s, d1r, d2s, d2r, s2, r2, cs, cr, gs, gr, qs, qr,
        os, orv, ags, agr, xr, mr,
        cv, wv, wbc, wo, sc_all, scs,
        gain_ref, gain_c, wdt_in, wdt_ref, so_in, so_ref, ocodes_ref, convx_ref, convb_ref,
        dtb_ref, rate_ref, skip_ref, ng_ref, hx0_ref, hb0_ref,
        l_sems, w_sems, cl_sem, st_sem, send_sem, v_sem, sc_sem, h_sem, d1_sem, d2_sem, sem2, c_sem,
        g_sem, q_sem, o_sem, a_sem, x_sem, f_sem,
    ):
        dp = lax.axis_index("dp")
        tp = lax.axis_index("tp")
        core = lax.rem(tp, 2)
        tp0 = tp - core
        mine = tp // 2
        sib = tp ^ 1
        group = tp // gsz
        member = tp - group * gsz
        half_t = tp // nb
        idx_t = tp - half_t * nb
        to_group = idx_t // per
        slot_t = half_t * per + lax.rem(idx_t, per)
        flat = dp * ntp + tp
        last_owner = flat // ndp
        last_slot = lax.rem(flat, ndp)
        sources = [tp * ndp + i for i in range(ndp)]
        pending = []

        def remote(src, dst, rsem, d, t):
            return pltpu.make_async_remote_copy(
                src_ref=src, dst_ref=dst, send_sem=send_sem, recv_sem=rsem,
                device_id=(d, t), device_id_type=MESH,
            )

        def send(src, dst, rsem, d, t):
            copy = remote(src, dst, rsem, d, t)
            copy.start()
            pending.append(copy)

        def recv(src, dst, rsem):
            remote(src, dst, rsem, dp, tp).wait_recv()

        def chunk(i):
            return pl.ds(pl.multiple_of(i * dc, LANES), dc)

        def columns(ti, par, ct):
            return pl.ds(pl.multiple_of((2 * ti + par) * lc + ct * LANES, LANES), LANES)

        small_loads = [
            (hid_hbm, hown), (hid_hbm.at[:, :, chunk(dp)], hrecv.at[dp]),
            (gain_hbm, gain_ref), (gain_hbm.at[:, chunk(dp)], gain_c),
            (sc_hbm, sc_all.at[mine]), (wdt_hbm, wdt_in), (so_hbm, so_in),
            (convx_hbm, convx_ref), (convb_hbm, convb_ref), (dtb_hbm, dtb_ref),
            (rate_hbm, rate_ref), (skip_hbm, skip_ref), (ng_hbm, ng_ref), (hx0_hbm, hx0_ref),
            (hb0_hbm, hb0_ref),
        ]
        small_loads = [
            pltpu.make_async_copy(a, b, l_sems.at[i]) for i, (a, b) in enumerate(small_loads)
        ]
        for copy in small_loads:
            copy.start()
        own_codes = []
        for k in list(range(1, nt2)) + [0]:
            ti = lax.rem(mine + k, nt2)
            for ct in range(nchunk):
                copy = pltpu.make_async_copy(
                    codes_hbm.at[:, :, columns(ti, core, ct)], cv.at[ti, core, ct],
                    cl_sem.at[k, ct],
                )
                copy.start()
                own_codes.append(copy)
        load_bc = pltpu.make_async_copy(wbc_hbm, wbc, w_sems.at[0])
        load_bc.start()

        barrier = pltpu.get_barrier_semaphore()

        def greet(d, t):
            pl.semaphore_signal(barrier, inc=1, device_id=(d, t), device_id_type=MESH)

        greeted = ntp - 1 + (ndp - 1) * gsz
        for k in range(1, ndp):
            for m in range(gsz):
                greet(lax.rem(dp + k, ndp), group * gsz + lax.rem(member + m, gsz))
        for k in range(1, ntp):
            greet(dp, tp ^ k)
        for f in sources:

            @pl.when(f != flat)
            def _(f=f):
                greet(f // ntp, lax.rem(f, ntp))

        @pl.when(last_owner == tp)
        def _():
            pl.semaphore_wait(barrier, greeted + ndp - 1)

        @pl.when(last_owner != tp)
        def _():
            pl.semaphore_wait(barrier, greeted + ndp)

        for k in range(1, nt2):
            ti = lax.rem(mine + k, nt2)
            send(sc_hbm, sc_all.at[mine], sc_sem.at[k], dp, 2 * ti + core)
        for k in range(1, ndp):
            peer = lax.rem(dp + k, ndp)
            send(hid_hbm.at[:, :, chunk(peer)], hrecv.at[dp], h_sem.at[k], peer, tp)
        for k in list(range(1, nt2)) + [0]:
            ti = lax.rem(mine + k, nt2)
            for ct in range(nchunk):
                send(
                    codes_hbm.at[:, :, columns(ti, 1 - core, ct)], cv.at[ti, core, ct],
                    v_sem.at[k, ct], dp, sib,
                )
        load_w = []
        for ct in range(nchunk):
            copy = pltpu.make_async_copy(
                wzx_hbm.at[pl.ds(dp * dc, dc), :, pl.ds(ct * LANES, LANES)], wv.at[ct],
                w_sems.at[1 + ct],
            )
            copy.start()
            load_w.append(copy)
        load_st = []
        for r in range(rows):
            copy = pltpu.make_async_copy(state_hbm.at[r], state.at[r], st_sem.at[r])
            copy.start()
            load_st.append(copy)
        load_out = pltpu.make_async_copy(
            wout_hbm.at[:, pl.ds(pl.multiple_of(dp * dc, LANES), dc)], wo, w_sems.at[1 + nchunk]
        )
        load_out.start()
        load_oc = pltpu.make_async_copy(ocodes_hbm, ocodes_ref, w_sems.at[2 + nchunk])
        load_oc.start()

        for copy in small_loads:
            copy.wait()
        wdt_ref[...] = jnp.concatenate(
            [wdt_in[...].astype(F32), jnp.zeros((LANES - heads, feats), F32)], axis=0
        ).astype(BF16)
        hx[0:3] = hx0_ref[...].astype(F32)
        hb[0:3] = hb0_ref[...].astype(F32)
        power = jnp.exp2(so_in[...].astype(F32))
        for b in range(lc // BLK):
            so_ref[b] = jnp.concatenate(
                [jnp.broadcast_to(power[b, :, c : c + 1], (1, BLK)) for c in range(dc // BLK)],
                axis=1,
            )

        def pick(value, slot):
            got = value[:, slot * rpd : (slot + 1) * rpd]
            for i in range(1, nt2):
                at = (2 * i + slot) * rpd
                got = jnp.where(mine == i, value[:, at : at + rpd], got)
            return got

        for slot in range(2):
            gp[slot] = pick(gain_c[...], slot)
        for k in range(1, nt2):
            frm = lax.rem(mine + nt2 - k, nt2)
            recv(sc_hbm, sc_all.at[frm], sc_sem.at[k])
        for ti in range(nt2):
            for slot in range(2):
                power = jnp.exp2(sc_all[ti, (tp0 + slot) * rpd // BLK].astype(F32))
                scs[ti, slot] = jnp.concatenate(
                    [jnp.broadcast_to(power[:, c : c + 1], (2, BLK)) for c in range(lc // BLK)],
                    axis=1,
                )
        for k in range(1, ndp):
            frm = lax.rem(dp + ndp - k, ndp)
            recv(hrecv.at[frm], hrecv.at[frm], h_sem.at[k])
        for s in range(steps):
            x = jnp.concatenate([hrecv[d, s].astype(F32) for d in range(ndp)], axis=0)
            for slot in range(2):
                hp[s, slot] = pick(x, slot)

        lane = lax.broadcasted_iota(jnp.int32, (rows, LANES), 1)

        def placer(width):
            row = lax.broadcasted_iota(jnp.int32, (width, 4 * width), 0)
            col = lax.broadcasted_iota(jnp.int32, (width, 4 * width), 1)
            want = jnp.where(col < 2 * width, 2 * row, 2 * row + 1 + 2 * width)
            return (col == want).astype(BF16)

        def spread(y, place):
            width = place.shape[0]
            n, count = y.shape[0], y.shape[1] // width
            if count > 1:
                y = jnp.concatenate(
                    [y[:, i * width : (i + 1) * width] for i in range(count)], axis=0
                )
            wide = jnp.dot(y, place, preferred_element_type=F32).astype(BF16)
            halves = [
                jnp.concatenate(
                    [
                        wide[i * n : (i + 1) * n, h * 2 * width : (h + 1) * 2 * width]
                        for i in range(count)
                    ],
                    axis=1,
                )
                for h in range(2)
            ]
            return jnp.concatenate(halves, axis=0)

        place_w = placer(LANES)
        place_c = place_w if rpd == LANES else placer(rpd)
        wr = wv.reshape(nchunk, 2 * dc, LANES)
        cvr = cv.reshape(nt2, 2, nchunk, 2 * rpd, LANES)
        skips = []
        for j in range(nchunk):
            v = jnp.zeros((rows, LANES), F32)
            for i in range(hpc):
                h = j * hpc + i
                inside = (lane >= i * psize) & (lane < (i + 1) * psize)
                v = jnp.where(inside, skip_ref[:, h : h + 1], v)
            skips.append(v)
        skip = jnp.concatenate(skips, axis=1)
        row_n = lax.broadcasted_iota(jnp.int32, (rows, nstate), 0)

        keep = jnp.ones((rows, lc), F32)
        added = []
        bmats = []
        for s in range(steps):
            if s > 0:
                recv(ags.at[0], agr.at[s - 1, sib], a_sem.at[s - 1, 1])
            spreads = []
            for slot in range(2):
                x = hp[s, slot]
                if s > 0:
                    x = x + jnp.concatenate(
                        [agr[s - 1, tp0 + slot, d].astype(F32) for d in range(ndp)], axis=0
                    )
                spreads.append(spread((x * gp[slot]).astype(BF16), place_c))
            width = min(256, lc)
            for k in list(range(1, nt2)) + [0]:
                ti = lax.rem(mine + k, nt2)
                if s == 0:
                    for ct in range(nchunk):
                        pltpu.make_async_copy(
                            codes_hbm.at[:, :, columns(ti, core, ct)], cv.at[ti, core, ct],
                            cl_sem.at[k, ct],
                        ).wait()
                        recv(
                            cv.at[ti, 1 - core, ct], cv.at[ti, 1 - core, ct], v_sem.at[k, ct]
                        )
                if s == 0:
                    for c in range(0, lc, width):
                        parts = []
                        for slot in range(2):
                            w = jnp.concatenate(
                                [
                                    cvr[ti, slot, ct]
                                    for ct in range(c // LANES, (c + width) // LANES)
                                ],
                                axis=1,
                            )
                            p = jnp.dot(spreads[slot], w, preferred_element_type=F32)
                            parts.append(
                                [
                                    p[h * allr : (h + 1) * allr]
                                    * scs[ti, slot, h : h + 1, c : c + width]
                                    for h in range(2)
                                ]
                            )
                        for h in range(2):
                            p = parts[0][h] + parts[1][h]
                            for d in range(ndp):
                                d1s[s, ti, d, :, h * lc + c : h * lc + c + width] = p[
                                    d * rows : (d + 1) * rows
                                ].astype(BF16)
                else:
                    for c in range(0, lc, width):
                        p = None
                        for slot in range(2):
                            w = jnp.concatenate(
                                [
                                    cvr[ti, slot, ct]
                                    for ct in range(c // LANES, (c + width) // LANES)
                                ],
                                axis=1,
                            )
                            q = jnp.dot(spreads[slot], w, preferred_element_type=F32)
                            p = q if p is None else p + q
                        for h in range(2):
                            for d in range(ndp):
                                d1s[s, ti, d, :, h * lc + c : h * lc + c + width] = p[
                                    h * allr + d * rows : h * allr + (d + 1) * rows
                                ].astype(BF16)
                for m in range(1, ndp):
                    peer = lax.rem(dp + m, ndp)
                    send(d1s.at[s, ti, peer], d1r.at[s, ti, m], d1_sem.at[s, ti, m], peer, tp)

            if s > 0:
                for k in range(2, ntp):
                    recv(ags.at[0], agr.at[s - 1, tp ^ k], a_sem.at[s - 1, k])
            x = jnp.concatenate([hrecv[d, s].astype(F32) for d in range(ndp)], axis=0)
            if s > 0:
                x = x + jnp.concatenate(
                    [
                        jnp.concatenate(
                            [agr[s - 1, t, d].astype(F32) for d in range(ndp)], axis=0
                        )
                        for t in range(ntp)
                    ],
                    axis=1,
                )
            wide = spread((x * gain_c[...]).astype(BF16), place_w)
            if s == 0:
                for copy in load_w:
                    copy.wait()
            for c in range(0, lc, width):
                w = jnp.concatenate(
                    [wr[ct] for ct in range(c // LANES, (c + width) // LANES)], axis=1
                )
                p = jnp.dot(wide, w, preferred_element_type=F32)
                for h in range(2):
                    for d in range(ndp):
                        s2[s, d, :, h * lc + c : h * lc + c + width] = p[
                            h * allr + d * rows : h * allr + (d + 1) * rows
                        ].astype(BF16)
            for k in range(1, ndp):
                peer = lax.rem(dp + k, ndp)
                send(s2.at[s, peer], r2.at[s, k], sem2.at[s, k], peer, tp)

            xo = hown[s].astype(F32)
            if s > 0:
                for k in range(1, ndp):
                    frm = lax.rem(dp + ndp - k, ndp)
                    for m in range(ntp):
                        recv(xr.at[s - 1, frm, tp ^ m], xr.at[s - 1, frm, tp ^ m],
                             x_sem.at[s - 1, k, m])
                for t in range(ntp):
                    xr[s - 1, dp, t] = agr[s - 1, t, dp]
                xo = xo + jnp.concatenate(
                    [xr[s - 1, d, t].astype(F32) for d in range(ndp) for t in range(ntp)], axis=1
                )
            inv = lax.rsqrt(jnp.sum(xo * xo, axis=1, keepdims=True) / feats + EPS)
            yo = (xo * gain_ref[...]).astype(BF16)
            if s == 0:
                load_bc.wait()
            hb[s + 3] = jnp.dot(yo, wbc[...], preferred_element_type=F32) * inv
            mixed = convb_ref[4:5, :]
            for i in range(4):
                mixed = mixed + hb[s + i] * convb_ref[i : i + 1, :]
            piece = silu(mixed)
            cs[s] = piece
            for m in range(gsz):
                target = to_group * gsz + m

                @pl.when(target != tp)
                def _(s=s, target=target):
                    remote(
                        cs.at[s], cr.at[s, slot_t], c_sem.at[s, slot_t], dp, target
                    ).start()

                @pl.when(target == tp)
                def _(s=s, piece=piece):
                    cr[s, slot_t] = piece

            z = lax.dot_general(
                yo, wdt_ref[...], (((1,), (1,)), ((), ())), preferred_element_type=F32
            )
            z = z[:, :heads] * inv + dtb_ref[...]
            dt = jnp.maximum(z, 0.0) + jnp.log1p(jnp.exp(-jnp.abs(z)))
            decay = jnp.exp(-dt * rate_ref[...])

            delta = None
            for k in list(range(1, nt2)) + [0]:
                ti = lax.rem(mine + k, nt2)
                total = d1s[s, ti, dp].astype(F32)
                for m in range(1, ndp):
                    recv(d1s.at[s, ti, 0], d1r.at[s, ti, m], d1_sem.at[s, ti, m])
                    total = total + d1r[s, ti, m].astype(F32)
                if k > 0:
                    d2s[s, k] = total.astype(BF16)
                    send(d2s.at[s, k], d2r.at[s, k], d2_sem.at[s, k], dp, 2 * ti + core)
                else:
                    delta = total

            if s == 0:
                load_out.wait()
                load_oc.wait()

                @pl.loop(0, lc // 32)
                def _(i):
                    at = pl.ds(pl.multiple_of(i * 32, 32), 32)
                    change = ocodes_ref[at, :].astype(F32) * so_ref[i // (BLK // 32)]
                    wo[at, :] = (wo[at, :].astype(F32) + change).astype(BF16)

                for r in range(rows):
                    load_st[r].wait()

                    @pl.loop(0, nchunk)
                    def _(j, r=r):
                        at = pl.ds(pl.multiple_of(j * LANES, LANES), LANES)
                        sb[at, r * nstate : (r + 1) * nstate] = state[r, at].astype(BF16)

            for q in range(2 * per):
                frm = (q // per) * nb + group * per + q % per

                @pl.when(frm != tp)
                def _(s=s, q=q):
                    recv(cs.at[s], cr.at[s, q], c_sem.at[s, q])

            bmat = [cr[s, i] for i in range(per)]
            cmat = [cr[s, per + i] for i in range(per)]
            bmat = bmat[0] if per == 1 else jnp.concatenate(bmat, axis=1)
            cmat = cmat[0] if per == 1 else jnp.concatenate(cmat, axis=1)
            bst_ref[s] = bmat
            bmats.append(bmat)
            high = cmat.astype(BF16).astype(F32)
            low = cmat - high
            query = jnp.concatenate(
                [
                    jnp.concatenate(
                        [jnp.where(row_n == r, v, 0.0) for r in range(rows)], axis=1
                    )
                    for v in (high, low)
                ],
                axis=0,
            ).astype(BF16)
            reads = []
            for c in range(0, lc, width):
                q = lax.dot_general(
                    query, sb[c : c + width, :], (((1,), (1,)), ((), ())),
                    preferred_element_type=F32,
                )
                reads.append(q[:rows] + q[rows:])
            reads = jnp.concatenate(reads, axis=1)

            total = delta + s2[s, dp].astype(F32)
            for k in range(1, ndp):
                recv(s2.at[s, 0], r2.at[s, k], sem2.at[s, k])
                total = total + r2[s, k].astype(F32)
            for k in range(1, nt2):
                recv(d2s.at[s, 0], d2r.at[s, k], d2_sem.at[s, k])
                total = total + d2r[s, k].astype(F32)
            hx[s + 3] = total[:, lc:] * inv
            mixed = convx_ref[4:5, :]
            for i in range(4):
                mixed = mixed + hx[s + i] * convx_ref[i : i + 1, :]
            inner = silu(mixed)
            dte, dece = [], []
            for j in range(nchunk):
                a = jnp.zeros((rows, LANES), F32)
                b = jnp.zeros((rows, LANES), F32)
                for i in range(hpc):
                    h = j * hpc + i
                    inside = (lane >= i * psize) & (lane < (i + 1) * psize)
                    a = jnp.where(inside, dt[:, h : h + 1], a)
                    b = jnp.where(inside, decay[:, h : h + 1], b)
                dte.append(a)
                dece.append(b)
            dte = jnp.concatenate(dte, axis=1)
            dece = jnp.concatenate(dece, axis=1)
            keep = keep * dece
            added = [v * dece for v in added] + [dte * inner]
            read = keep * reads + skip * inner
            for v, b in zip(added, bmats):
                read = read + v * jnp.sum(b * cmat, axis=1, keepdims=True)
            gated = read * silu(total[:, :lc] * inv)
            square = jnp.broadcast_to(
                jnp.sum(gated * gated, axis=1, keepdims=True), (rows, LANES)
            )
            qs[s] = square
            high = square.astype(BF16)
            gs[s, :, :lc] = (gated * ng_ref[...]).astype(BF16)
            gs[s, :, lc : lc + LANES] = high
            gs[s, :, lc + LANES :] = (square - high.astype(F32)).astype(BF16)
            for k in range(1, ndp):
                send(gs.at[s], gr.at[s, dp], g_sem.at[s, k], lax.rem(dp + k, ndp), tp)
            for k in list(range(1, ndp)) + [0]:
                for m in range(1, gsz):
                    send(
                        qs.at[s], qr.at[s, dp, member], q_sem.at[s, k, m],
                        lax.rem(dp + k, ndp), group * gsz + lax.rem(member + m, gsz),
                    )
            gr[s, dp] = gs[s]
            if s == steps - 1:
                for j in range(nchunk):
                    here = slice(j * LANES, (j + 1) * LANES)
                    coef_ref[j] = jnp.concatenate(
                        [keep[:, here]] + [v[:, here] for v in added], axis=0
                    )
            for k in range(ndp):
                frm_d = lax.rem(dp + ndp - k, ndp)
                if k > 0:
                    recv(gs.at[s], gr.at[s, frm_d], g_sem.at[s, k])
                for m in range(1, gsz):
                    frm = lax.rem(member + gsz - m, gsz)
                    recv(qs.at[s], qr.at[s, frm_d, frm], q_sem.at[s, k, m])
            every = jnp.concatenate(
                [gr[s, d, :, :lc].astype(F32) for d in range(ndp)], axis=0
            ).astype(BF16)
            scales = []
            for d in range(ndp):
                sq = gr[s, d, :, lc : lc + LANES].astype(F32)
                sq = sq + gr[s, d, :, lc + LANES :].astype(F32)
                for m in range(1, gsz):
                    sq = sq + qr[s, d, lax.rem(member + m, gsz)]
                scales.append(lax.rsqrt(sq[:, :1] / (di // G) + EPS))
            scale = jnp.concatenate(scales, axis=0)
            wide_o = max(ac, min(256, dc))
            for c in range(0, dc, wide_o):
                p = jnp.dot(every, wo[:, c : c + wide_o], preferred_element_type=F32) * scale
                for i in range(wide_o // ac):
                    os[s, c // ac + i] = p[:, i * ac : (i + 1) * ac].astype(BF16)
            for k in range(1, ntp):
                peer = tp ^ k
                send(os.at[s, peer], orv.at[s, k], o_sem.at[s, k], dp, peer)
            if s == 0:
                even = lax.rem(lax.broadcasted_iota(jnp.int32, (2 * rpd, LANES), 0), 2) == 0
                for ti in range(nt2):
                    for slot in range(2):
                        for ct in range(nchunk):
                            at = slice(ct * LANES, (ct + 1) * LANES)
                            by = jnp.where(even, scs[ti, slot, 0:1, at], scs[ti, slot, 1:2, at])
                            cvr[ti, slot, ct] = cvr[ti, slot, ct] * by.astype(BF16)
            total = os[s, tp].astype(F32)
            for k in range(1, ntp):
                recv(os.at[s, 0], orv.at[s, k], o_sem.at[s, k])
                total = total + orv[s, k].astype(F32)
            for d in range(ndp):
                ags[s, d] = total[d * rows : (d + 1) * rows].astype(BF16)
            if s < steps - 1:
                for k in range(1, ntp):
                    send(ags.at[s], agr.at[s, tp], a_sem.at[s, k], dp, tp ^ k)
                for k in range(1, ndp):
                    peer = lax.rem(dp + k, ndp)
                    for m in range(ntp):
                        send(
                            ags.at[s, peer], xr.at[s, dp, tp], x_sem.at[s, k, m], peer, tp ^ m
                        )
                agr[s, tp] = ags[s]

        def final(d):
            return remote(
                ags.at[steps - 1, d], mr.at[last_slot], f_sem.at[last_slot], d, last_owner
            )

        for k in range(ndp):
            d = lax.rem(dp + k, ndp)
            if k > 0:
                final(d).start()
            else:

                @pl.when(last_owner != tp)
                def _():
                    final(d).start()

                @pl.when(last_owner == tp)
                def _():
                    mr[last_slot] = ags[steps - 1, dp]

        for s in range(steps - 1):
            out_ref[s] = jnp.concatenate(
                [xr[s, f // ntp, lax.rem(f, ntp)].astype(F32) for f in sources], axis=1
            ).astype(BF16)
        for i, f in enumerate(sources):

            @pl.when(f != flat)
            def _(i=i):
                recv(mr.at[i], mr.at[i], f_sem.at[i])

        out_ref[steps - 1] = jnp.concatenate(
            [mr[i].astype(F32) for i in range(ndp)], axis=1
        ).astype(BF16)

        for copy in pending:
            copy.wait_send()
        for s in range(steps):
            for m in range(gsz):
                target = to_group * gsz + m

                @pl.when(target != tp)
                def _(s=s, target=target):
                    remote(
                        cs.at[s], cr.at[s, slot_t], c_sem.at[s, slot_t], dp, target
                    ).wait_send()

        for k in range(ndp):
            d = lax.rem(dp + k, ndp)
            if k > 0:
                final(d).wait_send()
            else:

                @pl.when(last_owner != tp)
                def _():
                    final(d).wait_send()

    vm = pltpu.VMEM
    dma = pltpu.SemaphoreType.DMA
    scratch = [
        vm((rows, lc, nstate), F32),
        vm((lc, rows * nstate), BF16),
        vm((steps + 3, rows, lc), F32),
        vm((steps + 3, rows, cb), F32),
        vm((steps, rows, feats), BF16),
        vm((ndp, steps, rows, dc), BF16),
        vm((steps, 2, allr, rpd), F32),
        vm((2, 1, rpd), F32),
        vm((steps, nt2, ndp, rows, 2 * lc), BF16),
        vm((steps, nt2, ndp, rows, 2 * lc), BF16),
        vm((steps, nt2, rows, 2 * lc), BF16),
        vm((steps, nt2, rows, 2 * lc), BF16),
        vm((steps, ndp, rows, 2 * lc), BF16),
        vm((steps, ndp, rows, 2 * lc), BF16),
        vm((steps, rows, cb), F32),
        vm((steps, 2 * per, rows, cb), F32),
        vm((steps, rows, lc + 2 * LANES), BF16),
        vm((steps, ndp, rows, lc + 2 * LANES), BF16),
        vm((steps, rows, LANES), F32),
        vm((steps, ndp, gsz, rows, LANES), F32),
        vm((steps, ntp, allr, ac), BF16),
        vm((steps, ntp, allr, ac), BF16),
        vm((steps, ndp, rows, ac), BF16),
        vm((steps, ntp, ndp, rows, ac), BF16),
        vm((steps, ndp, ntp, rows, ac), BF16),
        vm((ndp, rows, ac), BF16),
        vm((nt2, 2, nchunk, rpd, 2, LANES), BF16),
        vm((nchunk, dc, 2, LANES), BF16),
        vm((feats, cb), BF16),
        vm((lc, dc), BF16),
        vm((nt2, nkb, 2, lc // BLK), jnp.int32),
        vm((nt2, 2, 2, lc), F32),
        vm((1, feats), F32),
        vm((1, dc), F32),
        vm((heads, feats), BF16),
        vm((LANES, feats), BF16),
        vm((lc // BLK, 1, dc // BLK), jnp.int32),
        vm((lc // BLK, 1, dc), F32),
        vm((lc, dc), BF16),
        vm((5, lc), F32),
        vm((5, cb), F32),
        vm((1, heads), F32),
        vm((1, heads), F32),
        vm((1, heads), F32),
        vm((1, lc), F32),
        vm((3, rows, lc), BF16),
        vm((3, rows, cb), BF16),
        dma((15,)),
        dma((3 + nchunk,)),
        dma((nt2, nchunk)),
        dma((rows,)),
        dma(()),
        dma((nt2, nchunk)),
        dma((nt2,)),
        dma((ndp,)),
        dma((steps, nt2, ndp)),
        dma((steps, nt2)),
        dma((steps, ndp)),
        dma((steps, 2 * per)),
        dma((steps, ndp)),
        dma((steps, ndp, gsz)),
        dma((steps, ntp)),
        dma((steps, ntp)),
        dma((steps, ndp, ntp)),
        dma((ndp,)),
    ]
    vspec = pl.BlockSpec(memory_space=pltpu.VMEM)
    hspec = pl.BlockSpec(memory_space=pl.ANY)
    return pl.pallas_call(
        kernel,
        out_shape=(
            jax.ShapeDtypeStruct((steps, rows, oc), BF16),
            jax.ShapeDtypeStruct((nchunk, (1 + steps) * rows, LANES), F32),
            jax.ShapeDtypeStruct((steps, rows, nstate), F32),
        ),
        in_specs=[hspec] * 19,
        out_specs=(vspec, vspec, vspec),
        scratch_shapes=scratch,
        compiler_params=pltpu.CompilerParams(
            collective_id=0, has_side_effects=True, vmem_limit_bytes=60 * 1024 * 1024
        ),
    )


def make_update(steps, rows, nchunk, nstate, oc):
    count = steps * rows
    depth = -(-(rows + 3 * count) // LANES) * LANES
    rest = depth - rows - 3 * count

    def kernel(
        state_hbm, coef_hbm, bst_hbm, mixed_hbm, new_hbm, out_hbm,
        old, new, coef, bst, mixed, rhs, load_sem, store_sem, small_sem,
    ):
        small = [(coef_hbm, coef), (bst_hbm, bst), (mixed_hbm, mixed)]
        small = [
            pltpu.make_async_copy(a, b, small_sem.at[i]) for i, (a, b) in enumerate(small)
        ]
        for copy in small:
            copy.start()
        loads = [
            pltpu.make_async_copy(state_hbm.at[:, j], old.at[:, j], load_sem.at[j])
            for j in range(nchunk)
        ]
        for copy in loads:
            copy.start()
        for copy in small:
            copy.wait()
        stores = [pltpu.make_async_copy(mixed, out_hbm, small_sem.at[3])]
        stores[0].start()
        b = jnp.concatenate([bst[s] for s in range(steps)], axis=0)
        row = lax.rem(lax.broadcasted_iota(jnp.int32, (count, nstate), 0), rows)
        for r in range(rows):
            v = jnp.where(row == r, b, 0.0)
            high = v.astype(BF16).astype(F32)
            parts = [jnp.zeros((rows, nstate), F32), high, high, v - high]
            if rest:
                parts.append(jnp.zeros((rest, nstate), F32))
            rhs[:, r * nstate : (r + 1) * nstate] = jnp.concatenate(parts, axis=0).astype(BF16)
        for j in range(nchunk):
            keep = coef[j, :rows]
            added = coef[j, rows:]
            high = added.astype(BF16).astype(F32)
            parts = [keep, high, added - high, high]
            if rest:
                parts.append(jnp.zeros((rest, LANES), F32))
            full = jnp.concatenate(parts, axis=0).T
            lhs = full.astype(BF16)
            loads[j].wait()
            for r in range(rows):
                u = jnp.dot(
                    lhs, rhs[:, r * nstate : (r + 1) * nstate], preferred_element_type=F32
                )
                new[r, j] = full[:, r : r + 1] * old[r, j] + u
            copy = pltpu.make_async_copy(new.at[:, j], new_hbm.at[:, j], store_sem.at[j])
            copy.start()
            stores.append(copy)
        for copy in stores:
            copy.wait()

    vm = pltpu.VMEM
    hspec = pl.BlockSpec(memory_space=pl.ANY)
    return pl.pallas_call(
        kernel,
        out_shape=(
            jax.ShapeDtypeStruct((rows, nchunk, LANES, nstate), F32),
            jax.ShapeDtypeStruct((steps, rows, oc), BF16),
        ),
        in_specs=[hspec] * 4,
        out_specs=(hspec, hspec),
        scratch_shapes=[
            vm((rows, nchunk, LANES, nstate), F32),
            vm((rows, nchunk, LANES, nstate), F32),
            vm((nchunk, (1 + steps) * rows, LANES), F32),
            vm((steps, rows, nstate), F32),
            vm((steps, rows, oc), BF16),
            vm((depth, rows * nstate), BF16),
            pltpu.SemaphoreType.DMA((nchunk,)),
            pltpu.SemaphoreType.DMA((nchunk,)),
            pltpu.SemaphoreType.DMA((4,)),
        ],
        compiler_params=pltpu.CompilerParams(vmem_limit_bytes=60 * 1024 * 1024),
    )


def body(
    hidden_in, pre_gain, w_zx, zx_codes, zx_exponents, w_bc, w_dt, conv_x, conv_bc, dt_bias,
    decay_rate, skip_gain, conv_state_x, conv_state_bc, ssm_state, norm_gain, w_out, out_codes,
    out_exponents,
):
    ndp, ntp = lax.axis_size("dp"), lax.axis_size("tp")
    steps, rows, feats = hidden_in.shape
    dc = feats // ndp
    lc = w_zx.shape[2]
    cb = w_bc.shape[1]
    _, heads, psize, nstate = ssm_state.shape
    gsz = ntp // G
    di = lc * ntp

    call = make_kernel(ndp, ntp, steps, rows, dc, lc, cb, heads, psize, nstate, gsz, feats, di)
    mixed, coef, bst = call(
        hidden_in, pre_gain[None], w_dt.T, zx_exponents, out_exponents[:, None], out_codes, conv_x,
        conv_bc, dt_bias[None], decay_rate[None], skip_gain[None], norm_gain[None],
        conv_state_x.transpose(1, 0, 2), conv_state_bc.transpose(1, 0, 2),
        ssm_state.reshape(rows, lc, nstate),
        zx_codes, w_zx, w_bc, w_out,
    )
    update = make_update(steps, rows, lc // LANES, nstate, feats // ntp)
    state, out = update(
        ssm_state.reshape(rows, lc // LANES, LANES, nstate), coef, bst, mixed
    )
    return out, state.reshape(ssm_state.shape)


def solution(mesh):
    return jax.shard_map(
        body,
        mesh=mesh,
        in_specs=(
            P(None, "dp", None),
            P(),
            P(None, None, "tp"),
            P(("dp", "tp"), None, None),
            P("dp", None, "tp"),
            P(None, "tp"),
            P(None, "tp"),
            P(None, "tp"),
            P(None, "tp"),
            P("tp"),
            P("tp"),
            P("tp"),
            P("dp", None, "tp"),
            P("dp", None, "tp"),
            P("dp", "tp", None, None),
            P("tp"),
            P("tp", None),
            P("tp", "dp"),
            P("tp", "dp"),
        ),
        out_specs=(P(None, "dp", "tp"), P("dp", "tp", None, None)),
        check_vma=False,
    )
```
